32 devices in a mesh: area: 4 (over y, core), pos: 8 (over z, x).
Axes of the slice: x: 2, y: 2, z: 4, core: 2. Of those that a mesh axis runs over, the one named last changes fastest.
Arguments:
- exit_wave: bfloat16 [128, 2, 128, 128], P(('area', 'pos')), may hold values from -6 to 6
- amplitude: bfloat16 [128, 128, 128], P(('area', 'pos')), may hold values from 0.19921875 to 5
- probe: float32 [2, 128, 128], replicated, may hold values from -4 to 4
- offsets: int32 [128, 2], P(('area', 'pos')), may hold values from 0 to 127
- owner: int32 [128, 1], P(('area', 'pos')), may hold values from 0 to 7; in each aligned block of 4 rows (0 to 3, 4 to 7, ...) at most 2 rows name the same one
Outputs:
- new_wave: bfloat16 [128, 2, 128, 128], P(('area', 'pos'))
- object_field: float32 [2, 512, 1024], P(None, 'area', 'pos')
The draws below stay inside these ranges and needn't reach their ends.
Inputs may be any that keep to these rules, and one draw needn't show every extreme that they name: owner names the object tile column that holds the position's patch centre; of the 4 positions of one device at most 2 name the same tile.
All inputs are finite; a program needn't handle non-finite values.
Results may differ from the reference program's by a relative error of at most 0.0059.
Values may be sent and summed in bfloat16 or wider, within the bound.
No kernel may reach another device: no remote copies, remote signals or barrier semaphores. Data moves between devices by JAX's collectives and lax.ppermute only.
A program may use at most 64 MiB of HBM per device.

```python
import math
import jax
import jax.numpy as jnp
import numpy as np
from jax import lax

F = 128
TS = 128
C = 2
K = 4
POS = 128
NR = 512
NC = 1024
N_POS = 8


def set_ends(drawn, rng, smallest, largest):
    longest = drawn.shape.index(max(drawn.shape))
    spots = []
    for shift in (0, 1):
        where = [jax.random.randint(jax.random.fold_in(rng, axis), (), 0, length) for axis, length in enumerate(drawn.shape)]
        where[longest] = (where[longest] + shift) % drawn.shape[longest]
        spots.append(tuple(where))
    return drawn.at[spots[0]].set(smallest).at[spots[1]].set(largest)


def steps_of(rng, shape, cuts, low, high):
    def one(axis_at, shards_of):
        draws = jax.random.uniform(jax.random.fold_in(jax.random.fold_in(rng, 6), axis_at), (shards_of,), jnp.float32, low / len(cuts), high / len(cuts))
        return jnp.repeat(jnp.exp(draws), shape[axis_at] // shards_of).reshape((-1,) + (1,) * (len(shape) - axis_at - 1))

    loudness = one(*cuts[0])
    for cut in cuts[1:]:
        loudness = loudness * one(*cut)
    return loudness


def assign_block(stream_key, own, number, rows, number_of, top, most, lean):
    ranking = jax.random.permutation(stream_key, number_of)
    crowded, ordinary = shares(number_of, rows * top, most, lean, True), shares(number_of, rows * top, most, lean, False)
    places = jnp.arange(number_of)

    def named(lengths, rotation):
        used = int((lengths > 0).sum())
        fixed = max(1, used // 4)
        passed = fixed + (places - fixed + rotation * (used - fixed)) % max(1, number_of - fixed)
        return jnp.zeros((number_of,), jnp.int32).at[ranking[jnp.where(places < fixed, places, passed)]].set(jnp.asarray(lengths, jnp.int32))

    lengths = jnp.where(number % 4 == 0, named(crowded, number // 4), named(ordinary, number - number // 4 - 1))
    mixed = jax.random.permutation(jax.random.fold_in(own, 3), number_of)
    source_of, taker = mixed[0:number_of // 2 * 2:2], mixed[1:number_of // 2 * 2:2]
    room = jnp.minimum(lengths[source_of] - 1, most - lengths[taker]) // 2
    room = jnp.where((source_of == ranking[0]) | (taker == ranking[0]) | (lengths[taker] == 0), 0, jnp.maximum(room, 0))
    passed = jax.random.randint(jax.random.fold_in(own, 4), (number_of // 2,), 0, 1 << 20) % (room + 1)
    lengths = lengths.at[source_of].add(-passed).at[taker].add(passed)
    labels = jnp.searchsorted(jnp.cumsum(lengths), jnp.arange(rows * top), side="right").astype(jnp.int32)
    listing = labels.reshape(top, rows).T
    listing = listing[jax.random.permutation(jax.random.fold_in(own, 1), rows)]
    rotation = jax.random.randint(jax.random.fold_in(own, 2), (rows, 1), 0, top)
    return jnp.take_along_axis(listing, (jnp.arange(top)[None, :] + rotation) % top, axis=1)


def shares(amount, total, limit, skew, full):
    portions = [(1 << 20) // math.isqrt(standing ** skew) + 1 for standing in range(1, amount + 1)]
    largest = limit if full else min(limit, max(-(-total // amount), total * portions[0] // sum(portions)))
    least = 1 if total - largest >= amount - 1 else 0
    given, rest = [largest] + [least] * (amount - 1), total - largest - least * (amount - 1)
    while rest > 0:
        movable = [i for i in range(1, amount) if given[i] < largest] or [i for i in range(1, amount) if given[i] < limit]
        mass, remaining = sum([portions[i] for i in movable]), rest
        for i in movable:
            more = min(limit - given[i], max(1, remaining * portions[i] // mass), rest)
            given[i] = given[i] + more
            rest = rest - more
    return np.array(given)


def noise(rng, dims, spread, limit, split=(), kind=jnp.bfloat16):
    level = steps_of(rng, dims, split, -0.22, 0.18) if split else 1.0
    result = jax.random.normal(rng, dims, jnp.float32) * spread * level
    return jnp.minimum(jnp.maximum(result, -limit), limit).astype(kind)


def setup_inputs(seed: int = 0) -> dict:
    keys = jax.random.split(jax.random.key(seed), 6)
    exit_wave = noise(keys[0], (POS, 2, F, F), 1.0, 6.0, ((0, 32),))
    amplitude = jnp.clip(jnp.exp(math.log(5.0) - 3.2227897 * jax.random.uniform(keys[1], (POS, F, F), jnp.float32) ** steps_of(keys[1], (POS, F, F), ((0, 32),), -0.2, 0.2)), 0.19921875, 5.0).astype(jnp.bfloat16)
    probe = noise(keys[2], (2, F, F), 0.7, 4.0, (), jnp.float32)
    offsets = set_ends(jax.random.randint(keys[3], (POS, 2), 0, TS), jax.random.fold_in(keys[3], 1), 0, TS - 1).astype(jnp.int32)
    owner_keys = jax.random.split(jax.random.fold_in(keys[4], 1), POS // K)
    owner_turns = jax.random.permutation(jax.random.fold_in(keys[4], 3), POS // K)
    owner = jax.vmap(lambda own, number: assign_block(jax.random.fold_in(keys[4], 2), own, number, K, N_POS, 1, C, 1))(owner_keys, owner_turns).reshape((POS, 1))
    return dict(exit_wave=exit_wave, amplitude=amplitude, probe=probe, offsets=offsets, owner=owner)


def reference(exit_wave, amplitude, probe, offsets, owner):
    total = exit_wave.shape[0]
    margin = F // 2
    area_of = (jnp.arange(total, dtype=jnp.int32) // (K * N_POS)).astype(jnp.int32)
    rows_at = (area_of * TS + offsets[:, 0]).astype(jnp.int32)
    cols_at = (owner[:, 0] * TS + offsets[:, 1]).astype(jnp.int32)
    probe_re = probe[0]
    probe_im = probe[1]
    power_map = probe_re * probe_re + probe_im * probe_im

    def add_one(index, canvas):
        wave = lax.dynamic_index_in_dim(exit_wave, index, 0, keepdims=False).astype(jnp.float32)
        contrib_re = (probe_re * wave[0] + probe_im * wave[1]).astype(jnp.bfloat16).astype(jnp.float32)
        contrib_im = (probe_re * wave[1] - probe_im * wave[0]).astype(jnp.bfloat16).astype(jnp.float32)
        piece = jnp.stack([contrib_re, contrib_im, power_map], 0)
        where = (jnp.int32(0), rows_at[index], cols_at[index])
        old = lax.dynamic_slice(canvas, where, (3, F, F))
        return lax.dynamic_update_slice(canvas, old + piece, where)
    canvas = lax.fori_loop(0, total, add_one, jnp.zeros((3, NR + F, NC + F), jnp.float32))
    inner = canvas[:, margin:margin + NR, margin:margin + NC]
    object_field = inner[0:2] / (inner[2] + 0.1)[None]
    padded = jnp.pad(object_field.astype(jnp.bfloat16), ((0, 0), (margin, margin), (margin, margin)))

    def one_block(block):
        waves, amps, row_block, col_block = block
        patches = jax.vmap(lambda r, c: lax.dynamic_slice(padded, (jnp.int32(0), r, c), (2, F, F)))(row_block, col_block).astype(jnp.float32)
        wave_f = waves.astype(jnp.float32)
        proj_re = probe_re * patches[:, 0] - probe_im * patches[:, 1]
        proj_im = probe_re * patches[:, 1] + probe_im * patches[:, 0]
        trial = 2.0 * proj_re - wave_f[:, 0] + 1j * (2.0 * proj_im - wave_f[:, 1])
        spectrum = jnp.fft.fft2(trial, norm='ortho')
        modulus = jnp.sqrt(spectrum.real * spectrum.real + spectrum.imag * spectrum.imag + 0.01)
        fitted = amps.astype(jnp.float32) * spectrum / modulus
        back = jnp.fft.ifft2(fitted, norm='ortho')
        new_re = 0.75 * wave_f[:, 0] - 0.5 * proj_re + 0.75 * back.real
        new_im = 0.75 * wave_f[:, 1] - 0.5 * proj_im + 0.75 * back.imag
        return jnp.stack([new_re, new_im], 1).astype(jnp.bfloat16)
    groups = total // K
    blocks = (exit_wave.reshape(groups, K, 2, F, F), amplitude.reshape(groups, K, F, F), rows_at.reshape(groups, K), cols_at.reshape(groups, K))
    new_wave = lax.map(one_block, blocks).reshape(total, 2, F, F)
    return (new_wave, object_field)
```

```python
import functools
import math

import jax
import jax.numpy as jnp
import numpy as np
from jax import lax
from jax.experimental import pallas as pl
from jax.experimental.pallas import tpu as pltpu
from jax.sharding import PartitionSpec as P

F32 = jnp.float32
BF16 = jnp.bfloat16
VMEM = pl.BlockSpec(memory_space=pltpu.VMEM)
SMEM = pl.BlockSpec(memory_space=pltpu.SMEM)


def lanes_of(size):
    return lax.broadcasted_iota(jnp.int32, (size, size), 1)


def place(canvas, tile, channel, row, col, data):
    size = data.shape[0]
    turned = pltpu.roll(data, col, 1)
    right = lanes_of(size) < col
    rows = pl.ds(row, size)
    canvas[tile, channel, rows, :] += jnp.where(right, 0.0, turned)
    canvas[tile + 1, channel, rows, :] += jnp.where(right, turned, 0.0)


def cut(canvas, tile, channel, row, col, size):
    rows = pl.ds(row, size)
    here = canvas[tile, channel, rows, :]
    after = canvas[tile + 1, channel, rows, :]
    both = jnp.where(lanes_of(size) < col, after, here)
    return pltpu.roll(both, lax.rem(size - col, size), 1)


def tile_part(canvas, tile, channel, row, count, size):
    here = canvas[tile, channel, pl.ds(row, count), :]
    after = canvas[tile + 1, channel, pl.ds(row, count), :]
    half = size // 2
    lane = lax.broadcasted_iota(jnp.int32, (count, size), 1)
    return pltpu.roll(jnp.where(lane < half, after, here), half, 1)


def where_is(meta, device, number):
    return (meta[device, 3 * number], meta[device, 3 * number + 1], meta[device, 3 * number + 2])


def denom_kernel(areas, columns, held, size, meta, probe, denom, canvas):
    area = lax.axis_index("area")
    pos = lax.axis_index("pos")
    power = probe[0] * probe[0] + probe[1] * probe[1]
    canvas[...] = jnp.zeros_like(canvas)

    for shift in (-1, 0, 1):
        other = area + shift

        @pl.when((other >= 0) & (other < areas))
        def _(other=other, shift=shift):
            @pl.loop(0, columns)
            def _(source):
                for number in range(held):
                    row, col, tile = where_is(meta, other * columns + source, number)
                    place(canvas, tile, 0, row + (shift + 1) * size, col, power)

    me = area * columns + pos
    for number in range(held):
        row, col, tile = where_is(meta, me, number)
        denom[number] = cut(canvas, tile, 0, row + size, col, size)
    denom[held] = tile_part(canvas, pos, 0, size + size // 2, size, size)


def band_kernel(areas, columns, inner, held, size, sources, *refs):
    meta, probe = refs[:2]
    waves = refs[2 : 2 + len(sources)]
    own, up, down, canvas = refs[2 + len(sources) :]
    area = lax.axis_index("area")
    pos = lax.axis_index("pos")
    base = area * columns
    canvas[...] = jnp.zeros_like(canvas)
    probe_re = probe[0]
    probe_im = probe[1]
    for (steps, swapped), wave in zip(sources, waves):
        source = base + source_of(pos, steps, swapped, inner, columns)

        def add_one(number, carry, wave=wave, source=source):
            wave_re = wave[number, 0].astype(F32)
            wave_im = wave[number, 1].astype(F32)
            row, col, tile = where_is(meta, source, number)
            first = (probe_re * wave_re + probe_im * wave_im).astype(BF16).astype(F32)
            place(canvas, tile, 0, row + size, col, first)
            second = (probe_re * wave_im - probe_im * wave_re).astype(BF16).astype(F32)
            place(canvas, tile, 1, row + size, col, second)
            return carry

        lax.fori_loop(0, held, add_one, 0)
    half = size // 2
    for to, out in ((-1, up), (1, down)):
        device = jnp.clip(area + to, 0, areas - 1) * columns + pos
        for number in range(held):
            row, col, tile = where_is(meta, device, number)
            for channel in (0, 1):
                out[2 * number + channel] = cut(
                    canvas, tile, channel, row + (to + 1) * size, col, size
                ).astype(BF16)
        for channel in (0, 1):
            first = size if to < 0 else 2 * size + half
            out[2 * held, channel * half : (channel + 1) * half] = tile_part(
                canvas, pos, channel, first, half, size
            ).astype(BF16)
    for number in range(held):
        row, col, tile = where_is(meta, base + pos, number)
        for channel in (0, 1):
            own[2 * number + channel] = cut(canvas, tile, channel, row + size, col, size)
    for channel in (0, 1):
        own[2 * held + channel] = tile_part(canvas, pos, channel, size + half, size, size)


def split(value):
    high = value.astype(BF16)
    return (high, (value - high.astype(F32)).astype(BF16))


def times(left, right):
    def dot(a, b):
        return jnp.dot(a, b, preferred_element_type=F32)

    return dot(left[0], right[0]) + (dot(left[0], right[1]) + dot(left[1], right[0]))


def final_kernel(areas, columns, held, size, *refs):
    meta, own, above, below, denom, wave, amplitude, probe, twiddle = refs[:9]
    new_wave, tile_out = refs[9:]
    area = lax.axis_index("area")
    pos = lax.axis_index("pos")
    half = size // 2
    me = area * columns + pos
    scale = 1.0 / (denom[held] + 0.1)
    for channel in (0, 1):
        rows = slice(channel * half, (channel + 1) * half)
        sums = own[2 * held + channel]
        sums = sums + jnp.concatenate(
            [above[2 * held, rows].astype(F32), below[2 * held, rows].astype(F32)], 0
        )
        tile_out[channel] = sums * scale
    probe_re = probe[0]
    probe_im = probe[1]
    parts = [(twiddle[2 * i], twiddle[2 * i + 1]) for i in range(4)]
    row_at = lax.broadcasted_iota(jnp.int32, (size, size), 0)
    col_at = lax.broadcasted_iota(jnp.int32, (size, size), 1)
    for number in range(held):
        row, col, tile = where_is(meta, me, number)
        top = area * size + row - half
        left = tile * size + col - half
        inside = (
            (row_at >= -top)
            & (row_at < areas * size - top)
            & (col_at >= -left)
            & (col_at < columns * size - left)
        )
        share = jnp.where(inside, 1.0 / (denom[number] + 0.1), 0.0)
        patch = []
        for channel in (0, 1):
            at = 2 * number + channel
            sums = own[at] + (above[at].astype(F32) + below[at].astype(F32))
            patch.append((sums * share).astype(BF16).astype(F32))
        wave_re = wave[number, 0].astype(F32)
        wave_im = wave[number, 1].astype(F32)
        proj_re = probe_re * patch[0] - probe_im * patch[1]
        proj_im = probe_re * patch[1] + probe_im * patch[0]
        trial = jnp.concatenate([2.0 * proj_re - wave_re, 2.0 * proj_im - wave_im], 1)
        mid = times(split(trial), parts[0])
        mid = jnp.concatenate([mid[:, :size], mid[:, size:]], 0)
        spectrum = times(parts[1], split(mid))
        spec_re = spectrum[:size]
        spec_im = spectrum[size:]
        ratio = amplitude[number].astype(F32) * lax.rsqrt(
            spec_re * spec_re + spec_im * spec_im + 0.01
        )
        fitted = jnp.concatenate([spec_re * ratio, spec_im * ratio], 1)
        mid = times(split(fitted), parts[2])
        mid = jnp.concatenate([mid[:, :size], mid[:, size:]], 0)
        back = times(parts[3], split(mid))
        new_wave[number, 0] = (0.75 * wave_re - 0.5 * proj_re + 0.75 * back[:size]).astype(BF16)
        new_wave[number, 1] = (0.75 * wave_im - 0.5 * proj_im + 0.75 * back[size:]).astype(BF16)


def twiddles(size):
    at = np.arange(size)
    angle = 2.0 * math.pi * ((at[:, None] * at[None, :]) % size) / size
    real = np.cos(angle) / math.sqrt(size)
    imag = -np.sin(angle) / math.sqrt(size)
    kept = []
    for sign in (1.0, -1.0):
        im = sign * imag
        for whole in (np.block([[real, im], [-im, real]]), np.block([[real, -im], [im, real]])):
            whole = whole.astype(np.float32)
            high = whole.astype(BF16)
            kept += [high, (whole - high.astype(np.float32)).astype(BF16)]
    return np.stack(kept)


def source_of(pos, steps, swapped, inner, columns):
    source = lax.rem(pos + columns - inner * steps, columns)
    if swapped:
        source = source + 1 - 2 * lax.rem(source, 2)
    return source


def gathered(wave, columns):
    inner = 2 if columns % 2 == 0 else 1
    pieces = [((0, False), wave)]
    for steps in range(1, columns // inner):
        ring = [(i, (i + inner * steps) % columns) for i in range(columns)]
        pieces.append(((steps, False), lax.ppermute(wave, "pos", ring)))
    if inner == 2:
        pair = [(i, i ^ 1) for i in range(columns)]
        for (steps, _), piece in list(pieces):
            pieces.append(((steps, True), lax.ppermute(piece, "pos", pair)))
    return (inner, pieces)


def body(exit_wave, amplitude, probe, offsets, owner):
    areas = lax.axis_size("area")
    columns = lax.axis_size("pos")
    held = exit_wave.shape[0]
    size = exit_wave.shape[-1]
    inner, pieces = gathered(exit_wave, columns)
    mine = jnp.concatenate([offsets, owner], 1).reshape(1, 1, 3 * held)
    meta = lax.all_to_all(
        jnp.broadcast_to(mine, (areas * columns, 1, 3 * held)),
        ("area", "pos"),
        split_axis=0,
        concat_axis=0,
        tiled=True,
    ).reshape(areas * columns, 3 * held)

    denom = pl.pallas_call(
        functools.partial(denom_kernel, areas, columns, held, size),
        out_shape=jax.ShapeDtypeStruct((held + 1, size, size), F32),
        in_specs=[SMEM, VMEM],
        out_specs=VMEM,
        scratch_shapes=[pltpu.VMEM((columns + 1, 1, 4 * size, size), F32)],
        name="denominators",
    )(meta, probe)

    message = jax.ShapeDtypeStruct((2 * held + 1, size, size), BF16)
    own, up, down = pl.pallas_call(
        functools.partial(
            band_kernel, areas, columns, inner, held, size, tuple(k for k, _ in pieces)
        ),
        out_shape=(jax.ShapeDtypeStruct((2 * held + 2, size, size), F32), message, message),
        in_specs=[SMEM, VMEM] + [VMEM] * len(pieces),
        out_specs=(VMEM, VMEM, VMEM),
        scratch_shapes=[pltpu.VMEM((columns + 1, 2, 4 * size, size), F32)],
        name="band",
    )(meta, probe, *[piece for _, piece in pieces])

    below = lax.ppermute(up, "area", [(i + 1, i) for i in range(areas - 1)])
    above = lax.ppermute(down, "area", [(i, i + 1) for i in range(areas - 1)])

    return pl.pallas_call(
        functools.partial(final_kernel, areas, columns, held, size),
        out_shape=(
            jax.ShapeDtypeStruct(exit_wave.shape, BF16),
            jax.ShapeDtypeStruct((2, size, size), F32),
        ),
        in_specs=[SMEM] + [VMEM] * 8,
        out_specs=(VMEM, VMEM),
        name="relax",
    )(meta, own, above, below, denom, exit_wave, amplitude, probe, jnp.asarray(twiddles(size)))


def solution(mesh):
    return jax.shard_map(
        body,
        mesh=mesh,
        in_specs=(
            P(("area", "pos"), None, None, None),
            P(("area", "pos"), None, None),
            P(),
            P(("area", "pos"), None),
            P(("area", "pos"), None),
        ),
        out_specs=(P(("area", "pos"), None, None, None), P(None, "area", "pos")),
        check_vma=False,
    )
```

```python
import functools
import math

import jax
import jax.numpy as jnp
import numpy as np
from jax import lax
from jax.experimental import pallas as pl
from jax.experimental.pallas import tpu as pltpu
from jax.sharding import PartitionSpec as P


F32 = jnp.float32
BF16 = jnp.bfloat16
VMEM = pl.BlockSpec(memory_space=pltpu.VMEM)
SMEM = pl.BlockSpec(memory_space=pltpu.SMEM)


def lanes_of(rows, size):
    return lax.broadcasted_iota(jnp.int32, (rows, size), 1)


def where_is(meta, device, number):
    return tuple(meta[device, 3 * number + part] for part in range(3))


def place(canvas, tile, channel, row, col, data):
    size = data.shape[0]
    turned = pltpu.roll(data, col, 1)
    wraps = lanes_of(size, size) < col
    rows = pl.ds(row, size)
    canvas[tile, channel, rows, :] += jnp.where(wraps, 0.0, turned)
    canvas[tile + 1, channel, rows, :] += jnp.where(wraps, turned, 0.0)


def cut(canvas, tile, channel, row, col, size):
    rows = pl.ds(row, size)
    here = canvas[tile, channel, rows, :]
    after = canvas[tile + 1, channel, rows, :]
    both = jnp.where(lanes_of(size, size) < col, after, here)
    return pltpu.roll(both, lax.rem(size - col, size), 1)


def tile_part(canvas, tile, channel, row, count, size):
    here = canvas[tile, channel, pl.ds(row, count), :]
    after = canvas[tile + 1, channel, pl.ds(row, count), :]
    half = size // 2
    return pltpu.roll(jnp.where(lanes_of(count, size) < half, after, here), half, 1)


def stage_kernel(held, size, offsets, owner, probe, wave, payload):
    probe_re = probe[0]
    probe_im = probe[1]
    for number in range(held):
        wave_re = wave[number, 0].astype(F32)
        wave_im = wave[number, 1].astype(F32)
        for channel, part in (
            (0, probe_re * wave_re + probe_im * wave_im),
            (1, probe_re * wave_im - probe_im * wave_re),
        ):
            first = (2 * number + channel) * size
            payload[first : first + size, :] = part.astype(BF16)
    rows = payload.shape[0] - 2 * held * size
    row_at = lax.broadcasted_iota(jnp.int32, (rows, size), 0)
    col_at = lanes_of(rows, size)
    tail = jnp.zeros((rows, size), jnp.int32)
    for number in range(held):
        for part, value in enumerate((offsets[0, number], offsets[1, number], owner[0, number])):
            tail = jnp.where((row_at == number) & (col_at == part), value, tail)
    payload[2 * held * size :, :] = tail.astype(F32).astype(BF16)


def place_waves(canvas, held, size, waves, numbers, scalars, sem):
    for at, wave in enumerate(waves):
        numbers[at] = wave[2 * held * size :, :].astype(F32).astype(jnp.int32)
    copy = pltpu.make_async_copy(numbers, scalars, sem)
    copy.start()
    copy.wait()
    for at, wave in enumerate(waves):

        def add_one(number, carry, wave=wave, at=at):
            row = scalars[at, number, 0]
            col = scalars[at, number, 1]
            tile = scalars[at, number, 2]
            for channel in (0, 1):
                first = pl.multiple_of((2 * number + channel) * size, size)
                data = wave[pl.ds(first, size), :].astype(F32)
                place(canvas, tile, channel, row, col, data)
            return carry

        lax.fori_loop(0, held, add_one, 0)


def denominators(areas, columns, held, size, meta, probe, denom, canvas):
    area = lax.axis_index("area")
    pos = lax.axis_index("pos")
    power = probe[0] * probe[0] + probe[1] * probe[1]
    canvas[...] = jnp.zeros_like(canvas)

    for shift in (-1, 0, 1):
        other = area + shift

        @pl.when((other >= 0) & (other < areas))
        def _(other=other, shift=shift):
            @pl.loop(0, columns)
            def _(source):
                for number in range(held):
                    row, col, tile = where_is(meta, other * columns + source, number)
                    place(canvas, tile, 0, row + (shift + 1) * size, col, power)

    for number in range(held):
        row, col, tile = where_is(meta, area * columns + pos, number)
        denom[number] = cut(canvas, tile, 0, row + size, col, size)
    denom[held] = tile_part(canvas, pos, 0, size + size // 2, size, size)


def band_kernel(held, size, fresh, whole, *refs):
    waves = refs[:-4] if fresh else refs[:-5]
    canvas, numbers, scalars, sem = refs[-4:]
    if fresh:
        canvas[...] = jnp.zeros_like(canvas)
    elif not whole:
        canvas[...] = refs[-5][...]
    place_waves(canvas, held, size, waves, numbers, scalars, sem)


def late_kernel(areas, columns, held, size, whole, *refs):
    meta = refs[0]
    given, outer, paired, canvas, numbers, scalars, sem, shifted = refs[-8:]
    if not whole:
        canvas[...] = given[...]
    place_waves(canvas, held, size, refs[1:-8], numbers, scalars, sem)
    cut_messages(areas, columns, held, size, meta, canvas, outer, paired, shifted)


def neighbour(area, outer):
    step = 1 - 2 * lax.rem(area, 2)
    return -step if outer else step


def cut_messages(areas, columns, held, size, meta, canvas, outer, paired, shifted):
    area = lax.axis_index("area")
    pos = lax.axis_index("pos")
    half = size // 2
    for side in (0, 1):
        shifted[side, :size] = jnp.zeros((size, size), F32)
        shifted[side, 2 * size :] = jnp.zeros((size, size), F32)
    for out, is_outer in ((outer, True), (paired, False)):
        step = neighbour(area, is_outer)
        above = step < 0
        device = jnp.clip(area + step, 0, areas - 1) * columns + pos
        block = pl.multiple_of(jnp.where(above, 0, size), 8)
        for number in range(held):
            row, col, tile = where_is(meta, device, number)
            for channel in (0, 1):
                shifted[channel, size : 2 * size] = cut(canvas, tile, channel, block, col, size)
                first = jnp.where(above, row, row + size)
                out[2 * number + channel] = shifted[channel, pl.ds(first, size), :].astype(BF16)
        first = pl.multiple_of(jnp.where(above, 0, size + half), 8)
        for channel in (0, 1):
            out[2 * held, channel * half : (channel + 1) * half] = tile_part(
                canvas, pos, channel, first, half, size
            ).astype(BF16)


def own_kernel(columns, held, size, meta, canvas, own):
    pos = lax.axis_index("pos")
    me = lax.axis_index("area") * columns + pos
    for number in range(held):
        row, col, tile = where_is(meta, me, number)
        for channel in (0, 1):
            own[2 * number + channel] = cut(canvas, tile, channel, row, col, size)
    for channel in (0, 1):
        own[2 * held + channel] = tile_part(canvas, pos, channel, size // 2, size, size)


def split(value):
    high = value.astype(BF16)
    return (high, (value - high.astype(F32)).astype(BF16))


def from_right(data, matrix):
    high, low = data
    return jnp.dot(
        jnp.concatenate([high, low, high], 1), matrix, preferred_element_type=F32
    )


def from_left(matrix, data):
    high, low = data
    return jnp.dot(
        matrix, jnp.concatenate([high, low, high], 0), preferred_element_type=F32
    )


def to_columns(value, held, size):
    return jnp.concatenate(
        [
            jnp.concatenate(
                [
                    value[number * size : (number + 1) * size, part * size : (part + 1) * size]
                    for number in range(held)
                ],
                1,
            )
            for part in (0, 1)
        ],
        0,
    )


def final_kernel(areas, columns, held, size, *refs):
    meta, own, outer, paired, denom, wave, amplitude, probe, right, left = refs[:10]
    new_wave, tile_out, rows_high, rows_low, proj = refs[10:]
    area = lax.axis_index("area")
    pos = lax.axis_index("pos")
    half = size // 2
    me = area * columns + pos
    odd = lax.rem(area, 2) == 1
    scale = 1.0 / (denom[held] + 0.1)
    for channel in (0, 1):
        rows = slice(channel * half, (channel + 1) * half)
        sums = own[2 * held + channel]
        one = outer[2 * held, rows].astype(F32)
        two = paired[2 * held, rows].astype(F32)
        sums = sums + jnp.concatenate([jnp.where(odd, two, one), jnp.where(odd, one, two)], 0)
        tile_out[channel] = sums * scale
    probe_re = probe[0]
    probe_im = probe[1]
    row_at = lax.broadcasted_iota(jnp.int32, (size, size), 0)
    col_at = lanes_of(size, size)
    for number in range(held):
        row, col, tile = where_is(meta, me, number)
        top = area * size + row - half
        start = tile * size + col - half
        inside = (
            (row_at >= -top)
            & (row_at < areas * size - top)
            & (col_at >= -start)
            & (col_at < columns * size - start)
        )
        share = jnp.where(inside, 1.0 / (denom[number] + 0.1), 0.0)
        patch = []
        for channel in (0, 1):
            at = 2 * number + channel
            sums = own[at] + (outer[at].astype(F32) + paired[at].astype(F32))
            patch.append((sums * share).astype(BF16).astype(F32))
        proj_re = probe_re * patch[0] - probe_im * patch[1]
        proj_im = probe_re * patch[1] + probe_im * patch[0]
        proj[number, 0] = proj_re
        proj[number, 1] = proj_im
        at = slice(number * size, (number + 1) * size)
        for channel, part in ((0, proj_re), (1, proj_im)):
            high, low = split(2.0 * part - wave[number, channel].astype(F32))
            rows_high[at, channel * size : (channel + 1) * size] = high
            rows_low[at, channel * size : (channel + 1) * size] = low
    mid = to_columns(from_right((rows_high[...], rows_low[...]), right[0]), held, size)
    spectrum = from_left(left[0], split(mid))
    for number in range(held):
        at = slice(number * size, (number + 1) * size)
        spec_re = spectrum[:size, at]
        spec_im = spectrum[size:, at]
        ratio = amplitude[number].astype(F32) * lax.rsqrt(
            spec_re * spec_re + spec_im * spec_im + 0.01
        )
        for channel, part in ((0, spec_re), (1, spec_im)):
            high, low = split(part * ratio)
            rows_high[at, channel * size : (channel + 1) * size] = high
            rows_low[at, channel * size : (channel + 1) * size] = low
    mid = to_columns(from_right((rows_high[...], rows_low[...]), right[1]), held, size)
    back = from_left(left[1], split(mid))
    for number in range(held):
        at = slice(number * size, (number + 1) * size)
        for channel in (0, 1):
            new_wave[number, channel] = (
                0.75 * wave[number, channel].astype(F32)
                - 0.5 * proj[number, channel]
                + 0.75 * back[channel * size : (channel + 1) * size, at]
            ).astype(BF16)


def twiddles(size):
    at = np.arange(size)
    angle = 2.0 * math.pi * ((at[:, None] * at[None, :]) % size) / size
    real = np.cos(angle) / math.sqrt(size)
    imag = -np.sin(angle) / math.sqrt(size)

    def parts(whole, axis):
        whole = whole.astype(np.float32)
        high = whole.astype(BF16)
        low = (whole - high.astype(np.float32)).astype(BF16)
        return np.concatenate([high, high, low], axis)

    right = [parts(np.block([[real, im], [-im, real]]), 0) for im in (imag, -imag)]
    left = [parts(np.block([[real, -im], [im, real]]), 1) for im in (imag, -imag)]
    return (jnp.asarray(np.stack(right)), jnp.asarray(np.stack(left)))


def steps_of(lines):
    return sorted(range(1, lines), key=lambda step: (step != lines // 2, step))


def gathered(wave, columns):
    inner = 2 if columns % 2 == 0 else 1
    lines = columns // inner
    xor = lines & (lines - 1) == 0
    pieces = {(0, False): wave}
    for step in steps_of(lines):
        pairs = [
            (i, (i // inner ^ step if xor else (i // inner + step) % lines) * inner + i % inner)
            for i in range(columns)
        ]
        pieces[step, False] = lax.ppermute(wave, "pos", pairs)
    if inner == 2:
        for step in range(lines):
            pieces[step, True] = lax.ppermute(
                pieces[step, False], "pos", [(i, i ^ 1) for i in range(columns)]
            )
    return pieces


def on_chip(values):
    if sum(value.size * value.dtype.itemsize for value in values) > 2**23:
        return list(values)
    return [pltpu.with_memory_space_constraint(value, pltpu.VMEM) for value in values]


def limit(*values):
    held = sum(math.prod(value.shape) * np.dtype(value.dtype).itemsize for value in values)
    return pltpu.CompilerParams(vmem_limit_bytes=min(held + 2**23, 60 * 2**20))


SMALL = 6 * 2**20


def room(shape, dtype):
    if math.prod(shape) * np.dtype(dtype).itemsize <= SMALL:
        return pltpu.VMEM(shape, dtype)
    return jax.ShapeDtypeStruct(shape, dtype)


def body(exit_wave, amplitude, probe, offsets, owner):
    areas = lax.axis_size("area")
    columns = lax.axis_size("pos")
    held = exit_wave.shape[0]
    size = exit_wave.shape[-1]
    tail = -(-held // 16) * 16
    payload = pl.pallas_call(
        functools.partial(stage_kernel, held, size),
        out_shape=pltpu.VMEM((2 * held * size + tail, size), BF16),
        in_specs=[SMEM, SMEM, VMEM, VMEM],
        out_specs=VMEM,
        compiler_params=limit(probe, exit_wave),
        name="stage",
    )(
        *[
            pltpu.with_memory_space_constraint(value, pltpu.HBM)
            for value in (offsets.T, owner.T, probe, exit_wave)
        ]
    )
    pieces = gathered(payload, columns)
    mine = jnp.concatenate([offsets, owner], 1).reshape(1, 1, 3 * held)
    meta = lax.all_to_all(
        jnp.broadcast_to(mine, (areas * columns, 1, 3 * held)),
        ("area", "pos"),
        split_axis=0,
        concat_axis=0,
        tiled=True,
    ).reshape(areas * columns, 3 * held)

    powers = pltpu.VMEM((columns + 1, 1, 4 * size, size), F32)
    denom = pl.pallas_call(
        functools.partial(denominators, areas, columns, held, size),
        out_shape=room((held + 1, size, size), F32),
        in_specs=[SMEM, VMEM],
        out_specs=VMEM,
        scratch_shapes=[powers],
        compiler_params=limit(powers),
        name="denominators",
    )(meta, pltpu.with_memory_space_constraint(probe, pltpu.HBM))

    band = room((columns + 1, 2, 2 * size, size), F32)
    whole = not isinstance(band, jax.ShapeDtypeStruct)

    def scratch(count):
        return [
            pltpu.VMEM((count, tail, size), jnp.int32),
            pltpu.SMEM((count, tail, size), jnp.int32),
            pltpu.SemaphoreType.DMA,
        ]

    extra = [] if whole else [band, band]
    canvas = []
    for group in groups_of(pieces):
        waves = [pieces[kind] for kind in group]
        canvas = on_chip(canvas)
        canvas = [
            pl.pallas_call(
                functools.partial(band_kernel, held, size, not canvas, whole),
                out_shape=band,
                in_specs=[VMEM] * (len(waves) + len(canvas)),
                out_specs=VMEM,
                scratch_shapes=scratch(len(waves)),
                input_output_aliases={len(waves): 0} if canvas else {},
                compiler_params=limit(*extra, *([] if whole else waves)),
            )(*on_chip(waves), *canvas)
        ]
    message = room((2 * held + 1, size, size), BF16)
    waves = on_chip([list(pieces.values())[-1]])
    outer, paired, canvas = pl.pallas_call(
        functools.partial(late_kernel, areas, columns, held, size, whole),
        out_shape=(message, message, band),
        in_specs=[SMEM] + [VMEM] * 2,
        out_specs=(VMEM, VMEM, VMEM),
        scratch_shapes=scratch(1) + [pltpu.VMEM((2, 3 * size, size), F32)],
        input_output_aliases={2: 2},
        compiler_params=limit(*extra),
        name="band_late",
    )(meta, *waves, *on_chip(canvas))
    pairs = [(i, i + 1) for i in range(1, areas - 1, 2)]
    outer = lax.ppermute(outer, "area", pairs + [(b, a) for a, b in pairs])
    pairs = [(i, i + 1) for i in range(0, areas - 1, 2)]
    paired = lax.ppermute(paired, "area", pairs + [(b, a) for a, b in pairs])
    own = pl.pallas_call(
        functools.partial(own_kernel, columns, held, size),
        out_shape=room((2 * held + 2, size, size), F32),
        in_specs=[SMEM, VMEM],
        out_specs=VMEM,
        compiler_params=limit(*extra),
        name="own_sums",
    )(meta, *on_chip([canvas]))

    rows = pltpu.VMEM((held * size, 2 * size), BF16)
    proj = pltpu.VMEM((held, 2, size, size), F32)
    return pl.pallas_call(
        functools.partial(final_kernel, areas, columns, held, size),
        out_shape=(
            jax.ShapeDtypeStruct((held, 2, size, size), BF16),
            jax.ShapeDtypeStruct((2, size, size), F32),
        ),
        in_specs=[SMEM] + [VMEM] * 9,
        out_specs=(VMEM, VMEM),
        scratch_shapes=[rows, rows, proj],
        compiler_params=limit(rows, rows, proj, proj, proj, proj, proj),
        name="relax",
    )(
        meta,
        *on_chip([own, outer, paired, denom, exit_wave, amplitude, probe]),
        *on_chip(twiddles(size)),
    )


def groups_of(pieces):
    kinds = list(pieces)[:-1]
    if len(kinds) == 7:
        return [
            [(0, False), (0, True), (1, False), (2, False)],
            [(1, True), (3, False), (2, True)],
        ]
    return [kinds[at : at + 4] for at in range(0, len(kinds), 4)]


def solution(mesh):
    return jax.shard_map(
        body,
        mesh=mesh,
        in_specs=(
            P(("area", "pos"), None, None, None),
            P(("area", "pos"), None, None),
            P(),
            P(("area", "pos"), None),
            P(("area", "pos"), None),
        ),
        out_specs=(P(("area", "pos"), None, None, None), P(None, "area", "pos")),
        check_vma=False,
    )
```

```python
import functools
import math

import jax
import jax.numpy as jnp
import numpy as np
from jax import lax
from jax.experimental import pallas as pl
from jax.experimental.pallas import tpu as pltpu
from jax.sharding import PartitionSpec as P


F32 = jnp.float32
BF16 = jnp.bfloat16
VMEM = pl.BlockSpec(memory_space=pltpu.VMEM)
SMEM = pl.BlockSpec(memory_space=pltpu.SMEM)


def lanes_of(rows, size):
    return lax.broadcasted_iota(jnp.int32, (rows, size), 1)


def where_is(meta, device, number):
    return tuple(meta[device, 3 * number + part] for part in range(3))


def place(canvas, tile, channel, row, col, data):
    size = data.shape[0]
    turned = pltpu.roll(data, col, 1)
    wraps = lanes_of(size, size) < col
    rows = pl.ds(row, size)
    canvas[tile, channel, rows, :] += jnp.where(wraps, 0.0, turned)
    canvas[tile + 1, channel, rows, :] += jnp.where(wraps, turned, 0.0)


def cut(canvas, tile, channel, row, col, size):
    rows = pl.ds(row, size)
    here = canvas[tile, channel, rows, :]
    after = canvas[tile + 1, channel, rows, :]
    both = jnp.where(lanes_of(size, size) < col, after, here)
    return pltpu.roll(both, lax.rem(size - col, size), 1)


def tile_part(canvas, tile, channel, row, count, size):
    here = canvas[tile, channel, pl.ds(row, count), :]
    after = canvas[tile + 1, channel, pl.ds(row, count), :]
    half = size // 2
    return pltpu.roll(jnp.where(lanes_of(count, size) < half, after, here), half, 1)


def stage_kernel(held, size, offsets, owner, probe, wave, payload, *halves):
    probe_re = probe[0]
    probe_im = probe[1]
    for number in range(held):
        wave_re = wave[number, 0].astype(F32)
        wave_im = wave[number, 1].astype(F32)
        for channel, part in (
            (0, probe_re * wave_re + probe_im * wave_im),
            (1, probe_re * wave_im - probe_im * wave_re),
        ):
            first = (2 * number + channel) * size
            rounded = part.astype(BF16)
            payload[first : first + size, :] = rounded
            for half in halves:
                if 0 <= first < half.shape[0]:
                    half[first : first + size, :] = rounded
                first -= half.shape[0]
    rows = payload.shape[0] - 2 * held * size
    row_at = lax.broadcasted_iota(jnp.int32, (rows, size), 0)
    col_at = lanes_of(rows, size)
    tail = jnp.zeros((rows, size), jnp.int32)
    for number in range(held):
        for part, value in enumerate((offsets[0, number], offsets[1, number], owner[0, number])):
            tail = jnp.where((row_at == number) & (col_at == part), value, tail)
    payload[2 * held * size :, :] = tail.astype(F32).astype(BF16)


def add_waves(canvas, size, wave, first, count, where):
    def add_one(number, carry):
        row, col, tile = where(first + number)
        for channel in (0, 1):
            at = pl.multiple_of((2 * number + channel) * size, size)
            place(canvas, tile, channel, row, col, wave[pl.ds(at, size), :].astype(F32))
        return carry

    lax.fori_loop(0, count, add_one, 0, unroll=count <= 4)


def place_by_tail(canvas, held, size, waves, numbers, scalars, sem):
    for at, wave in enumerate(waves):
        numbers[at] = wave[2 * held * size :, :].astype(F32).astype(jnp.int32)
    copy = pltpu.make_async_copy(numbers, scalars, sem)
    copy.start()
    copy.wait()
    for at, wave in enumerate(waves):
        add_waves(
            canvas,
            size,
            wave,
            0,
            held,
            lambda number, at=at: tuple(scalars[at, number, part] for part in range(3)),
        )


def place_by_meta(canvas, columns, size, meta, specs, waves):
    inner = 2 if columns % 2 == 0 else 1
    base = lax.axis_index("area") * columns
    for (kind, first, count), wave in zip(specs, waves):
        source = base + source_of(lax.axis_index("pos"), kind, inner, columns)
        add_waves(
            canvas,
            size,
            wave,
            first,
            count,
            lambda number, source=source: where_is(meta, source, number),
        )


def source_of(pos, kind, inner, columns):
    step, swapped = kind
    line = pos // inner
    lines = columns // inner
    if lines & (lines - 1) == 0:
        line = jnp.bitwise_xor(line, step)
    else:
        line = lax.rem(line + lines - step, lines)
    side = lax.rem(pos, inner)
    return line * inner + (inner - 1 - side if swapped else side)


def place_powers(canvas, meta, probe, area, shift, columns, held, size):
    power = probe[0] * probe[0] + probe[1] * probe[1]

    @pl.loop(0, columns)
    def _(source):
        for number in range(held):
            row, col, tile = where_is(meta, area * columns + source, number)
            place(canvas, tile, 0, row + (shift + 1) * size, col, power)


def powers_kernel(columns, held, size, meta, probe, canvas):
    canvas[...] = jnp.zeros_like(canvas)
    place_powers(canvas, meta, probe, lax.axis_index("area"), 0, columns, held, size)


def denominators(areas, columns, held, size, whole, meta, probe, given, share, canvas):
    area = lax.axis_index("area")
    pos = lax.axis_index("pos")
    if not whole:
        canvas[...] = given[...]
    for shift in (-1, 1):
        other = area + shift

        @pl.when((other >= 0) & (other < areas))
        def _(other=other, shift=shift):
            place_powers(canvas, meta, probe, other, shift, columns, held, size)

    half = size // 2
    row_at = lax.broadcasted_iota(jnp.int32, (size, size), 0)
    col_at = lanes_of(size, size)
    for number in range(held):
        row, col, tile = where_is(meta, area * columns + pos, number)
        top = area * size + row - half
        start = tile * size + col - half
        inside = (
            (row_at >= -top)
            & (row_at < areas * size - top)
            & (col_at >= -start)
            & (col_at < columns * size - start)
        )
        sums = cut(canvas, tile, 0, row + size, col, size)
        share[number] = jnp.where(inside, 1.0 / (sums + 0.1), 0.0)
    share[held] = 1.0 / (tile_part(canvas, pos, 0, size + half, size, size) + 0.1)


def first_kernel(held, size, *refs):
    canvas, numbers, scalars, sem = refs[-4:]
    canvas[...] = jnp.zeros_like(canvas)
    place_by_tail(canvas, held, size, refs[:-4], numbers, scalars, sem)


def band_kernel(columns, size, whole, specs, meta, *refs):
    given, canvas = refs[-2:]
    if not whole:
        canvas[...] = given[...]
    place_by_meta(canvas, columns, size, meta, specs, refs[:-2])


def outer_kernel(areas, columns, held, size, whole, specs, meta, *refs):
    given, out, canvas, shifted = refs[-4:]
    if not whole:
        canvas[...] = given[...]
    place_by_meta(canvas, columns, size, meta, specs, refs[:-4])
    cut_message(areas, columns, held, size, meta, canvas, out, shifted, True)


def paired_kernel(areas, columns, held, size, meta, canvas, out, own, shifted):
    cut_message(areas, columns, held, size, meta, canvas, out, shifted, False)
    own_sums(columns, held, size, meta, canvas, own)


def neighbour(area, outer):
    step = 1 - 2 * lax.rem(area, 2)
    return -step if outer else step


def cut_message(areas, columns, held, size, meta, canvas, out, shifted, is_outer):
    area = lax.axis_index("area")
    pos = lax.axis_index("pos")
    half = size // 2
    for side in (0, 1):
        shifted[side, :size] = jnp.zeros((size, size), F32)
        shifted[side, 2 * size :] = jnp.zeros((size, size), F32)
    step = neighbour(area, is_outer)
    above = step < 0
    device = jnp.clip(area + step, 0, areas - 1) * columns + pos
    block = pl.multiple_of(jnp.where(above, 0, size), 8)
    for number in range(held):
        row, col, tile = where_is(meta, device, number)
        for channel in (0, 1):
            shifted[channel, size : 2 * size] = cut(canvas, tile, channel, block, col, size)
            first = jnp.where(above, row, row + size)
            out[2 * number + channel] = shifted[channel, pl.ds(first, size), :].astype(BF16)
    first = pl.multiple_of(jnp.where(above, 0, size + half), 8)
    for channel in (0, 1):
        out[2 * held, channel * half : (channel + 1) * half] = tile_part(
            canvas, pos, channel, first, half, size
        ).astype(BF16)


def own_sums(columns, held, size, meta, canvas, own):
    pos = lax.axis_index("pos")
    me = lax.axis_index("area") * columns + pos
    for number in range(held):
        row, col, tile = where_is(meta, me, number)
        for channel in (0, 1):
            own[2 * number + channel] = cut(canvas, tile, channel, row, col, size)
    for channel in (0, 1):
        own[2 * held + channel] = tile_part(canvas, pos, channel, size // 2, size, size)


def split(value):
    high = value.astype(BF16)
    return (high, (value - high.astype(F32)).astype(BF16))


def dot(left, right):
    return jnp.dot(left, right, preferred_element_type=F32)


def from_right(high, low, matrix):
    size = matrix.shape[1]
    if low is None:
        return dot(jnp.concatenate([high, high], 1), matrix[: 2 * size])
    return dot(jnp.concatenate([high, high, low], 1), matrix)


def from_left(matrix, high, low):
    size = matrix.shape[0]
    if low is None:
        return dot(matrix[:, : 2 * size], jnp.concatenate([high, high], 0))
    return dot(matrix, jnp.concatenate([high, high, low], 0))


def there(rows_high, rows_low, right, left, held, size, chunk):
    results = []
    for first in range(0, held, chunk):
        count = min(chunk, held - first)
        at = slice(first * size, (first + count) * size)
        low = None if rows_low is None else rows_low[at, :]
        mid = to_columns(from_right(rows_high[at, :], low, right), count, size)
        high = mid.astype(BF16)
        low = None if rows_low is None else (mid - high.astype(F32)).astype(BF16)
        results.append(from_left(left, high, low))
    return jnp.concatenate(results, 1)


def to_columns(value, held, size):
    return jnp.concatenate(
        [
            jnp.concatenate(
                [
                    value[number * size : (number + 1) * size, part * size : (part + 1) * size]
                    for number in range(held)
                ],
                1,
            )
            for part in (0, 1)
        ],
        0,
    )


def final_kernel(held, size, *refs):
    own, outer, paired, share, wave, amplitude, probe, right, left = refs[:9]
    new_wave, tile_out, rows_high, rows_low, proj = refs[9:]
    half = size // 2
    odd = lax.rem(lax.axis_index("area"), 2) == 1
    scale = share[held]
    for channel in (0, 1):
        rows = slice(channel * half, (channel + 1) * half)
        sums = own[2 * held + channel]
        one = outer[2 * held, rows].astype(F32)
        two = paired[2 * held, rows].astype(F32)
        sums = sums + jnp.concatenate([jnp.where(odd, two, one), jnp.where(odd, one, two)], 0)
        tile_out[channel] = sums * scale
    probe_re = probe[0]
    probe_im = probe[1]
    for number in range(held):
        patch = []
        for channel in (0, 1):
            at = 2 * number + channel
            sums = own[at] + (outer[at].astype(F32) + paired[at].astype(F32))
            patch.append((sums * share[number]).astype(BF16).astype(F32))
        proj_re = probe_re * patch[0] - probe_im * patch[1]
        proj_im = probe_re * patch[1] + probe_im * patch[0]
        proj[number, 0] = proj_re
        proj[number, 1] = proj_im
        at = slice(number * size, (number + 1) * size)
        for channel, part in ((0, proj_re), (1, proj_im)):
            high, low = split(2.0 * part - wave[number, channel].astype(F32))
            rows_high[at, channel * size : (channel + 1) * size] = high
            rows_low[at, channel * size : (channel + 1) * size] = low
    spectrum = there(rows_high, rows_low, right[0], left[0], held, size, CHUNK)
    for number in range(held):
        at = slice(number * size, (number + 1) * size)
        spec_re = spectrum[:size, at]
        spec_im = spectrum[size:, at]
        ratio = amplitude[number].astype(F32) * lax.rsqrt(
            spec_re * spec_re + spec_im * spec_im + 0.01
        )
        for channel, part in ((0, spec_re), (1, spec_im)):
            high, low = split(part * ratio)
            rows_high[at, channel * size : (channel + 1) * size] = high
            rows_low[at, channel * size : (channel + 1) * size] = low
    back = there(rows_high, rows_low, right[1], left[1], held, size, CHUNK)
    for number in range(held):
        at = slice(number * size, (number + 1) * size)
        for channel in (0, 1):
            new_wave[number, channel] = (
                0.75 * wave[number, channel].astype(F32)
                - 0.5 * proj[number, channel]
                + 0.75 * back[channel * size : (channel + 1) * size, at]
            ).astype(BF16)


def twiddles(size):
    at = np.arange(size)
    angle = 2.0 * math.pi * ((at[:, None] * at[None, :]) % size) / size
    real = np.cos(angle) / math.sqrt(size)
    imag = -np.sin(angle) / math.sqrt(size)

    def parts(whole, axis):
        whole = whole.astype(np.float32)
        high = whole.astype(BF16)
        low = (whole - high.astype(np.float32)).astype(BF16)
        return np.concatenate([high, low, high], axis)

    right = [parts(np.block([[real, im], [-im, real]]), 0) for im in (imag, -imag)]
    left = [parts(np.block([[real, -im], [im, real]]), 1) for im in (imag, -imag)]
    return (jnp.asarray(np.stack(right)), jnp.asarray(np.stack(left)))


def steps_of(lines):
    return sorted(range(1, lines), key=lambda step: (step != lines // 2, step))


def gathered(payload, halves, held, columns):
    inner = 2 if columns % 2 == 0 else 1
    lines = columns // inner
    xor = lines & (lines - 1) == 0
    steps = [0] + steps_of(lines)
    pieces = []

    def send(kind, parts, pairs):
        for first, count, value in parts:
            moved = lax.ppermute(value, "pos", pairs)
            pieces.append((kind, first, count, moved))

    for step in steps:
        pairs = [
            (i, (i // inner ^ step if xor else (i // inner + step) % lines) * inner + i % inner)
            for i in range(columns)
        ]
        parts = halves if step == steps[-1] else [(0, held, payload)]
        if step == 0:
            pieces.append(((0, False), 0, held, payload))
        else:
            send((step, False), parts, pairs)
    if inner == 2:
        pairs = [(i, i ^ 1) for i in range(columns)]
        for kind, *part in list(pieces):
            if xor and lines > 2 and kind[0] == 1:
                along = [(i, (i // inner ^ 1) * inner + i % inner) for i in range(columns)]
                moved = lax.ppermute(beside, "pos", along)
                pieces.append(((1, True), 0, held, moved))
                continue
            moved = lax.ppermute(part[2], "pos", pairs)
            if kind[0] == 0:
                beside = moved
            pieces.append(((kind[0], True), part[0], part[1], moved))
    return pieces


def on_chip(values):
    if sum(value.size * value.dtype.itemsize for value in values) > 2**23:
        return list(values)
    return [pltpu.with_memory_space_constraint(value, pltpu.VMEM) for value in values]


def limit(*values):
    held = sum(math.prod(value.shape) * np.dtype(value.dtype).itemsize for value in values)
    return pltpu.CompilerParams(vmem_limit_bytes=min(held + 2**23, 60 * 2**20))


SMALL = 6 * 2**20
CHUNK = 2


def room(shape, dtype):
    if math.prod(shape) * np.dtype(dtype).itemsize <= SMALL:
        return pltpu.VMEM(shape, dtype)
    return jax.ShapeDtypeStruct(shape, dtype)


def body(exit_wave, amplitude, probe, offsets, owner):
    areas = lax.axis_size("area")
    columns = lax.axis_size("pos")
    held = exit_wave.shape[0]
    size = exit_wave.shape[-1]
    tail = -(-held // 16) * 16
    cuts = [count for count in (held // 2, held - held // 2) if count]
    payload, *halves = pl.pallas_call(
        functools.partial(stage_kernel, held, size),
        out_shape=[room((2 * held * size + tail, size), BF16)]
        + [room((2 * count * size, size), BF16) for count in cuts],
        in_specs=[SMEM, SMEM, VMEM, VMEM],
        out_specs=[VMEM] * (1 + len(cuts)),
        compiler_params=limit(probe, exit_wave),
        name="stage",
    )(
        *[
            pltpu.with_memory_space_constraint(value, pltpu.HBM)
            for value in (offsets.T, owner.T, probe, exit_wave)
        ]
    )
    firsts = [0, cuts[0]]
    pieces = gathered(payload, list(zip(firsts, cuts, halves)), held, columns)
    mine = jnp.concatenate([offsets, owner], 1).reshape(1, 1, 3 * held)
    meta = lax.all_to_all(
        jnp.broadcast_to(mine, (areas * columns, 1, 3 * held)),
        ("area", "pos"),
        split_axis=0,
        concat_axis=0,
        tiled=True,
    ).reshape(areas * columns, 3 * held)

    powers = room((columns + 1, 1, 4 * size, size), F32)
    whole = not isinstance(powers, jax.ShapeDtypeStruct)
    far_probe = pltpu.with_memory_space_constraint(probe, pltpu.HBM)
    weights = pl.pallas_call(
        functools.partial(powers_kernel, columns, held, size),
        out_shape=powers,
        in_specs=[SMEM, VMEM],
        out_specs=VMEM,
        compiler_params=limit(*([] if whole else [powers])),
        name="powers",
    )(meta, far_probe)
    share, _ = pl.pallas_call(
        functools.partial(denominators, areas, columns, held, size, whole),
        out_shape=(room((held + 1, size, size), F32), powers),
        in_specs=[SMEM, VMEM, VMEM],
        out_specs=(VMEM, VMEM),
        input_output_aliases={2: 1},
        compiler_params=limit(*([] if whole else [powers, powers])),
        name="denominators",
    )(meta, far_probe, *on_chip([weights]))

    band = room((columns + 1, 2, 2 * size, size), F32)
    whole = not isinstance(band, jax.ShapeDtypeStruct)

    extra = [] if whole else [band, band]
    first, *groups, late = groups_of(pieces)
    waves = [piece[-1] for piece in first]
    canvas = pl.pallas_call(
        functools.partial(first_kernel, held, size),
        out_shape=band,
        in_specs=[VMEM] * len(waves),
        out_specs=VMEM,
        scratch_shapes=[
            pltpu.VMEM((len(waves), tail, size), jnp.int32),
            pltpu.SMEM((len(waves), tail, size), jnp.int32),
            pltpu.SemaphoreType.DMA,
        ],
        compiler_params=limit(*extra, *([] if whole else waves)),
        name="band0",
    )(*on_chip(waves))
    for group in groups:
        waves = [piece[-1] for piece in group]
        canvas = pl.pallas_call(
            functools.partial(band_kernel, columns, size, whole, [piece[:3] for piece in group]),
            out_shape=band,
            in_specs=[SMEM] + [VMEM] * (len(waves) + 1),
            out_specs=VMEM,
            input_output_aliases={len(waves) + 1: 0},
            compiler_params=limit(*extra, *([] if whole else waves)),
        )(meta, *on_chip(waves), *on_chip([canvas]))
    message = room((2 * held + 1, size, size), BF16)
    waves = [piece[-1] for piece in late]
    shifted = pltpu.VMEM((2, 3 * size, size), F32)
    outer, canvas = pl.pallas_call(
        functools.partial(
            outer_kernel, areas, columns, held, size, whole, [piece[:3] for piece in late]
        ),
        out_shape=(message, band),
        in_specs=[SMEM] + [VMEM] * (len(waves) + 1),
        out_specs=(VMEM, VMEM),
        scratch_shapes=[shifted],
        input_output_aliases={len(waves) + 1: 1},
        compiler_params=limit(*extra),
        name="band_outer",
    )(meta, *on_chip(waves), *on_chip([canvas]))
    pairs = [(i, i + 1) for i in range(1, areas - 1, 2)]
    outer = lax.ppermute(outer, "area", pairs + [(b, a) for a, b in pairs])
    paired, own = pl.pallas_call(
        functools.partial(paired_kernel, areas, columns, held, size),
        out_shape=(message, room((2 * held + 2, size, size), F32)),
        in_specs=[SMEM, VMEM],
        out_specs=(VMEM, VMEM),
        scratch_shapes=[shifted],
        compiler_params=limit(*extra),
        name="band_paired",
    )(meta, *on_chip([canvas]))
    pairs = [(i, i + 1) for i in range(0, areas - 1, 2)]
    paired = lax.ppermute(paired, "area", pairs + [(b, a) for a, b in pairs])

    rows = pltpu.VMEM((held * size, 2 * size), BF16)
    proj = pltpu.VMEM((held, 2, size, size), F32)
    return pl.pallas_call(
        functools.partial(final_kernel, held, size),
        out_shape=(
            jax.ShapeDtypeStruct((held, 2, size, size), BF16),
            jax.ShapeDtypeStruct((2, size, size), F32),
        ),
        in_specs=[VMEM] * 9,
        out_specs=(VMEM, VMEM),
        scratch_shapes=[rows, rows, proj],
        compiler_params=limit(rows, rows, proj, proj, proj, proj, proj),
        name="relax",
    )(
        *on_chip([own, outer, paired, share, exit_wave, amplitude, probe]),
        *on_chip(twiddles(size)),
    )


def groups_of(pieces):
    at = {(kind, first): piece for piece in pieces for kind, first in [piece[:2]]}
    if len(pieces) == 10:
        half = pieces[-1][1]
        order = [
            [((0, False), 0), ((0, True), 0), ((1, False), 0), ((2, False), 0)],
            [((1, True), 0), ((2, True), 0), ((3, False), 0), ((3, False), half)],
            [((3, True), 0), ((3, True), half)],
        ]
        return [[at[key] for key in group] for group in order]
    return [pieces[first : first + 4] for first in range(0, len(pieces), 4)]


def solution(mesh):
    return jax.shard_map(
        body,
        mesh=mesh,
        in_specs=(
            P(("area", "pos"), None, None, None),
            P(("area", "pos"), None, None),
            P(),
            P(("area", "pos"), None),
            P(("area", "pos"), None),
        ),
        out_specs=(P(("area", "pos"), None, None, None), P(None, "area", "pos")),
        check_vma=False,
    )
```

```python
import functools
import math

import jax
import jax.numpy as jnp
import numpy as np
from jax import lax
from jax.experimental import pallas as pl
from jax.experimental.pallas import tpu as pltpu
from jax.sharding import PartitionSpec as P


F32 = jnp.float32
BF16 = jnp.bfloat16
VMEM = pl.BlockSpec(memory_space=pltpu.VMEM)
SMEM = pl.BlockSpec(memory_space=pltpu.SMEM)


def lanes_of(rows, size):
    return lax.broadcasted_iota(jnp.int32, (rows, size), 1)


def where_is(meta, device, number):
    return tuple(meta[device, 3 * number + part] for part in range(3))


def place(canvas, tile, channel, row, col, data):
    size = data.shape[0]
    turned = pltpu.roll(data, col, 1)
    wraps = lanes_of(size, size) < col
    rows = pl.ds(row, size)
    canvas[tile, channel, rows, :] += jnp.where(wraps, 0.0, turned)
    canvas[tile + 1, channel, rows, :] += jnp.where(wraps, turned, 0.0)


def cut(canvas, tile, channel, row, col, size):
    rows = pl.ds(row, size)
    here = canvas[tile, channel, rows, :]
    after = canvas[tile + 1, channel, rows, :]
    both = jnp.where(lanes_of(size, size) < col, after, here)
    return pltpu.roll(both, lax.rem(size - col, size), 1)


def tile_part(canvas, tile, channel, row, count, size):
    here = canvas[tile, channel, pl.ds(row, count), :]
    after = canvas[tile + 1, channel, pl.ds(row, count), :]
    half = size // 2
    return pltpu.roll(jnp.where(lanes_of(count, size) < half, after, here), half, 1)


def stage_kernel(held, size, offsets, owner, probe, wave, payload):
    probe_re = probe[0]
    probe_im = probe[1]
    for number in range(held):
        wave_re = wave[number, 0].astype(F32)
        wave_im = wave[number, 1].astype(F32)
        for channel, part in (
            (0, probe_re * wave_re + probe_im * wave_im),
            (1, probe_re * wave_im - probe_im * wave_re),
        ):
            first = (2 * number + channel) * size
            payload[first : first + size, :] = part.astype(BF16)
    rows = payload.shape[0] - 2 * held * size
    row_at = lax.broadcasted_iota(jnp.int32, (rows, size), 0)
    col_at = lanes_of(rows, size)
    tail = jnp.zeros((rows, size), jnp.int32)
    for number in range(held):
        for part, value in enumerate((offsets[0, number], offsets[1, number], owner[0, number])):
            tail = jnp.where((row_at == number) & (col_at == part), value, tail)
    payload[2 * held * size :, :] = tail.astype(F32).astype(BF16)


def halve_kernel(payload, *halves):
    first = 0
    for half in halves:
        half[...] = payload[first : first + half.shape[0], :]
        first += half.shape[0]


def add_waves(canvas, size, wave, first, count, where):
    def add_one(number, carry):
        row, col, tile = where(first + number)
        for channel in (0, 1):
            at = pl.multiple_of((2 * number + channel) * size, size)
            place(canvas, tile, channel, row, col, wave[pl.ds(at, size), :].astype(F32))
        return carry

    lax.fori_loop(0, count, add_one, 0, unroll=count <= 4)


def place_by_tail(canvas, held, size, waves, numbers, scalars, sem):
    for at, wave in enumerate(waves):
        numbers[at] = wave[2 * held * size :, :].astype(F32).astype(jnp.int32)
    copy = pltpu.make_async_copy(numbers, scalars, sem)
    copy.start()
    copy.wait()
    for at, wave in enumerate(waves):
        add_waves(
            canvas,
            size,
            wave,
            0,
            held,
            lambda number, at=at: tuple(scalars[at, number, part] for part in range(3)),
        )


def place_by_meta(canvas, columns, size, meta, specs, waves):
    inner = 2 if columns % 2 == 0 else 1
    base = lax.axis_index("area") * columns
    for (kind, first, count), wave in zip(specs, waves):
        source = base + source_of(lax.axis_index("pos"), kind, inner, columns)
        add_waves(
            canvas,
            size,
            wave,
            first,
            count,
            lambda number, source=source: where_is(meta, source, number),
        )


def source_of(pos, kind, inner, columns):
    step, swapped = kind
    line = pos // inner
    lines = columns // inner
    if lines & (lines - 1) == 0:
        line = jnp.bitwise_xor(line, step)
    else:
        line = lax.rem(line + lines - step, lines)
    side = lax.rem(pos, inner)
    return line * inner + (inner - 1 - side if swapped else side)


def place_powers(canvas, meta, probe, area, shift, columns, held, size):
    power = probe[0] * probe[0] + probe[1] * probe[1]

    @pl.loop(0, columns)
    def _(source):
        for number in range(held):
            row, col, tile = where_is(meta, area * columns + source, number)
            place(canvas, tile, 0, row + (shift + 1) * size, col, power)


def powers_kernel(columns, held, size, meta, probe, canvas):
    canvas[...] = jnp.zeros_like(canvas)
    place_powers(canvas, meta, probe, lax.axis_index("area"), 0, columns, held, size)


def denominators(areas, columns, held, size, whole, meta, probe, given, share, canvas):
    area = lax.axis_index("area")
    pos = lax.axis_index("pos")
    if not whole:
        canvas[...] = given[...]
    for shift in (-1, 1):
        other = area + shift

        @pl.when((other >= 0) & (other < areas))
        def _(other=other, shift=shift):
            place_powers(canvas, meta, probe, other, shift, columns, held, size)

    half = size // 2
    row_at = lax.broadcasted_iota(jnp.int32, (size, size), 0)
    col_at = lanes_of(size, size)
    for number in range(held):
        row, col, tile = where_is(meta, area * columns + pos, number)
        top = area * size + row - half
        start = tile * size + col - half
        inside = (
            (row_at >= -top)
            & (row_at < areas * size - top)
            & (col_at >= -start)
            & (col_at < columns * size - start)
        )
        sums = cut(canvas, tile, 0, row + size, col, size)
        share[number] = jnp.where(inside, 1.0 / (sums + 0.1), 0.0)
    share[held] = 1.0 / (tile_part(canvas, pos, 0, size + half, size, size) + 0.1)


def first_kernel(held, size, *refs):
    canvas, numbers, scalars, sem = refs[-4:]
    canvas[...] = jnp.zeros_like(canvas)
    place_by_tail(canvas, held, size, refs[:-4], numbers, scalars, sem)


def band_kernel(columns, size, whole, specs, meta, *refs):
    given, canvas = refs[-2:]
    if not whole:
        canvas[...] = given[...]
    place_by_meta(canvas, columns, size, meta, specs, refs[:-2])


def outer_kernel(areas, columns, held, size, whole, specs, meta, *refs):
    given, out, canvas, shifted = refs[-4:]
    if not whole:
        canvas[...] = given[...]
    place_by_meta(canvas, columns, size, meta, specs, refs[:-4])
    cut_message(areas, columns, held, size, meta, canvas, out, shifted, True)


def paired_kernel(areas, columns, held, size, meta, canvas, out, own, shifted):
    cut_message(areas, columns, held, size, meta, canvas, out, shifted, False)
    own_sums(columns, held, size, meta, canvas, own)


def neighbour(area, outer):
    step = 1 - 2 * lax.rem(area, 2)
    return -step if outer else step


def cut_message(areas, columns, held, size, meta, canvas, out, shifted, is_outer):
    area = lax.axis_index("area")
    pos = lax.axis_index("pos")
    half = size // 2
    for side in (0, 1):
        shifted[side, :size] = jnp.zeros((size, size), F32)
        shifted[side, 2 * size :] = jnp.zeros((size, size), F32)
    step = neighbour(area, is_outer)
    above = step < 0
    device = jnp.clip(area + step, 0, areas - 1) * columns + pos
    block = pl.multiple_of(jnp.where(above, 0, size), 8)
    for number in range(held):
        row, col, tile = where_is(meta, device, number)
        for channel in (0, 1):
            shifted[channel, size : 2 * size] = cut(canvas, tile, channel, block, col, size)
            first = jnp.where(above, row, row + size)
            out[2 * number + channel] = shifted[channel, pl.ds(first, size), :].astype(BF16)
    first = pl.multiple_of(jnp.where(above, 0, size + half), 8)
    for channel in (0, 1):
        out[2 * held, channel * half : (channel + 1) * half] = tile_part(
            canvas, pos, channel, first, half, size
        ).astype(BF16)


def own_sums(columns, held, size, meta, canvas, own):
    pos = lax.axis_index("pos")
    me = lax.axis_index("area") * columns + pos
    for number in range(held):
        row, col, tile = where_is(meta, me, number)
        for channel in (0, 1):
            own[2 * number + channel] = cut(canvas, tile, channel, row, col, size)
    for channel in (0, 1):
        own[2 * held + channel] = tile_part(canvas, pos, channel, size // 2, size, size)


def split(value):
    high = value.astype(BF16)
    return (high, (value - high.astype(F32)).astype(BF16))


def dot(left, right):
    return jnp.dot(left, right, preferred_element_type=F32)


def from_right(high, low, matrix):
    size = matrix.shape[1]
    if low is None:
        return dot(jnp.concatenate([high, high], 1), matrix[: 2 * size])
    return dot(jnp.concatenate([high, high, low], 1), matrix)


def from_left(matrix, high, low):
    size = matrix.shape[0]
    if low is None:
        return dot(matrix[:, : 2 * size], jnp.concatenate([high, high], 0))
    return dot(matrix, jnp.concatenate([high, high, low], 0))


def there(rows_high, rows_low, right, left, held, size, chunk):
    results = []
    for first in range(0, held, chunk):
        count = min(chunk, held - first)
        at = slice(first * size, (first + count) * size)
        low = None if rows_low is None else rows_low[at, :]
        mid = to_columns(from_right(rows_high[at, :], low, right), count, size)
        high = mid.astype(BF16)
        low = None if rows_low is None else (mid - high.astype(F32)).astype(BF16)
        results.append(from_left(left, high, low))
    return jnp.concatenate(results, 1)


def to_columns(value, held, size):
    return jnp.concatenate(
        [
            jnp.concatenate(
                [
                    value[number * size : (number + 1) * size, part * size : (part + 1) * size]
                    for number in range(held)
                ],
                1,
            )
            for part in (0, 1)
        ],
        0,
    )


def final_kernel(held, size, *refs):
    own, outer, paired, share, wave, amplitude, probe, right, left = refs[:9]
    new_wave, tile_out, rows_high, rows_low, proj = refs[9:]
    half = size // 2
    odd = lax.rem(lax.axis_index("area"), 2) == 1
    scale = share[held]
    for channel in (0, 1):
        rows = slice(channel * half, (channel + 1) * half)
        sums = own[2 * held + channel]
        one = outer[2 * held, rows].astype(F32)
        two = paired[2 * held, rows].astype(F32)
        sums = sums + jnp.concatenate([jnp.where(odd, two, one), jnp.where(odd, one, two)], 0)
        tile_out[channel] = sums * scale
    probe_re = probe[0]
    probe_im = probe[1]
    for number in range(held):
        patch = []
        for channel in (0, 1):
            at = 2 * number + channel
            sums = own[at] + (outer[at].astype(F32) + paired[at].astype(F32))
            patch.append((sums * share[number]).astype(BF16).astype(F32))
        proj_re = probe_re * patch[0] - probe_im * patch[1]
        proj_im = probe_re * patch[1] + probe_im * patch[0]
        proj[number, 0] = proj_re
        proj[number, 1] = proj_im
        at = slice(number * size, (number + 1) * size)
        for channel, part in ((0, proj_re), (1, proj_im)):
            high, low = split(2.0 * part - wave[number, channel].astype(F32))
            rows_high[at, channel * size : (channel + 1) * size] = high
            rows_low[at, channel * size : (channel + 1) * size] = low
    spectrum = there(rows_high, rows_low, right[0], left[0], held, size, CHUNK)
    for number in range(held):
        at = slice(number * size, (number + 1) * size)
        spec_re = spectrum[:size, at]
        spec_im = spectrum[size:, at]
        ratio = amplitude[number].astype(F32) * lax.rsqrt(
            spec_re * spec_re + spec_im * spec_im + 0.01
        )
        for channel, part in ((0, spec_re), (1, spec_im)):
            high, low = split(part * ratio)
            rows_high[at, channel * size : (channel + 1) * size] = high
            rows_low[at, channel * size : (channel + 1) * size] = low
    back = there(rows_high, rows_low, right[1], left[1], held, size, CHUNK)
    for number in range(held):
        at = slice(number * size, (number + 1) * size)
        for channel in (0, 1):
            new_wave[number, channel] = (
                0.75 * wave[number, channel].astype(F32)
                - 0.5 * proj[number, channel]
                + 0.75 * back[channel * size : (channel + 1) * size, at]
            ).astype(BF16)


def twiddles(size):
    at = np.arange(size)
    angle = 2.0 * math.pi * ((at[:, None] * at[None, :]) % size) / size
    real = np.cos(angle) / math.sqrt(size)
    imag = -np.sin(angle) / math.sqrt(size)

    def parts(whole, axis):
        whole = whole.astype(np.float32)
        high = whole.astype(BF16)
        low = (whole - high.astype(np.float32)).astype(BF16)
        return np.concatenate([high, low, high], axis)

    right = [parts(np.block([[real, im], [-im, real]]), 0) for im in (imag, -imag)]
    left = [parts(np.block([[real, -im], [im, real]]), 1) for im in (imag, -imag)]
    return (jnp.asarray(np.stack(right)), jnp.asarray(np.stack(left)))


def steps_of(lines):
    return sorted(range(1, lines), key=lambda step: (step != lines // 2, step))


def gathered(payload, halves, held, columns):
    inner = 2 if columns % 2 == 0 else 1
    lines = columns // inner
    xor = lines & (lines - 1) == 0
    steps = [0] + steps_of(lines)
    pieces = []

    def send(kind, parts, pairs):
        for first, count, value in parts:
            moved = lax.ppermute(value, "pos", pairs)
            pieces.append((kind, first, count, moved))

    for step in steps:
        pairs = [
            (i, (i // inner ^ step if xor else (i // inner + step) % lines) * inner + i % inner)
            for i in range(columns)
        ]
        parts = halves if step == steps[-1] else [(0, held, payload)]
        if step == 0:
            pieces.append(((0, False), 0, held, payload))
        else:
            send((step, False), parts, pairs)
    if inner == 2:
        pairs = [(i, i ^ 1) for i in range(columns)]
        for kind, *part in list(pieces):
            if xor and lines > 2 and kind[0] == 1:
                along = [(i, (i // inner ^ 1) * inner + i % inner) for i in range(columns)]
                moved = lax.ppermute(beside, "pos", along)
                pieces.append(((1, True), 0, held, moved))
                continue
            moved = lax.ppermute(part[2], "pos", pairs)
            if kind[0] == 0:
                beside = moved
            pieces.append(((kind[0], True), part[0], part[1], moved))
    return pieces


def on_chip(values):
    if sum(value.size * value.dtype.itemsize for value in values) > 2**23:
        return list(values)
    return [pltpu.with_memory_space_constraint(value, pltpu.VMEM) for value in values]


def limit(*values):
    held = sum(math.prod(value.shape) * np.dtype(value.dtype).itemsize for value in values)
    return pltpu.CompilerParams(vmem_limit_bytes=min(held + 2**23, 60 * 2**20))


SMALL = 6 * 2**20
CHUNK = 2


def room(shape, dtype):
    if math.prod(shape) * np.dtype(dtype).itemsize <= SMALL:
        return pltpu.VMEM(shape, dtype)
    return jax.ShapeDtypeStruct(shape, dtype)


def body(exit_wave, amplitude, probe, offsets, owner):
    areas = lax.axis_size("area")
    columns = lax.axis_size("pos")
    held = exit_wave.shape[0]
    size = exit_wave.shape[-1]
    tail = -(-held // 16) * 16
    cuts = [count for count in (held // 2, held - held // 2) if count]
    payload = pl.pallas_call(
        functools.partial(stage_kernel, held, size),
        out_shape=room((2 * held * size + tail, size), BF16),
        in_specs=[SMEM, SMEM, VMEM, VMEM],
        out_specs=VMEM,
        compiler_params=limit(probe, exit_wave),
        name="stage",
    )(
        *[
            pltpu.with_memory_space_constraint(value, pltpu.HBM)
            for value in (offsets.T, owner.T, probe, exit_wave)
        ]
    )
    halves = pl.pallas_call(
        halve_kernel,
        out_shape=[room((2 * count * size, size), BF16) for count in cuts],
        in_specs=[VMEM],
        out_specs=[VMEM] * len(cuts),
        compiler_params=limit(payload, payload),
        name="halve",
    )(payload)
    firsts = [0, cuts[0]]
    pieces = gathered(payload, list(zip(firsts, cuts, halves)), held, columns)
    mine = jnp.concatenate([offsets, owner], 1).reshape(1, 1, 3 * held)
    meta = lax.all_to_all(
        jnp.broadcast_to(mine, (areas * columns, 1, 3 * held)),
        ("area", "pos"),
        split_axis=0,
        concat_axis=0,
        tiled=True,
    ).reshape(areas * columns, 3 * held)

    powers = room((columns + 1, 1, 4 * size, size), F32)
    whole = not isinstance(powers, jax.ShapeDtypeStruct)
    far_probe = pltpu.with_memory_space_constraint(probe, pltpu.HBM)
    weights = pl.pallas_call(
        functools.partial(powers_kernel, columns, held, size),
        out_shape=powers,
        in_specs=[SMEM, VMEM],
        out_specs=VMEM,
        compiler_params=limit(*([] if whole else [powers])),
        name="powers",
    )(meta, far_probe)
    share, _ = pl.pallas_call(
        functools.partial(denominators, areas, columns, held, size, whole),
        out_shape=(room((held + 1, size, size), F32), powers),
        in_specs=[SMEM, VMEM, VMEM],
        out_specs=(VMEM, VMEM),
        input_output_aliases={2: 1},
        compiler_params=limit(*([] if whole else [powers, powers])),
        name="denominators",
    )(meta, far_probe, *on_chip([weights]))

    band = room((columns + 1, 2, 2 * size, size), F32)
    whole = not isinstance(band, jax.ShapeDtypeStruct)

    extra = [] if whole else [band, band]
    first, *groups, late = groups_of(pieces)
    waves = [piece[-1] for piece in first]
    canvas = pl.pallas_call(
        functools.partial(first_kernel, held, size),
        out_shape=band,
        in_specs=[VMEM] * len(waves),
        out_specs=VMEM,
        scratch_shapes=[
            pltpu.VMEM((len(waves), tail, size), jnp.int32),
            pltpu.SMEM((len(waves), tail, size), jnp.int32),
            pltpu.SemaphoreType.DMA,
        ],
        compiler_params=limit(*extra, *([] if whole else waves)),
        name="band0",
    )(*on_chip(waves))
    for group in groups:
        waves = [piece[-1] for piece in group]
        canvas = pl.pallas_call(
            functools.partial(band_kernel, columns, size, whole, [piece[:3] for piece in group]),
            out_shape=band,
            in_specs=[SMEM] + [VMEM] * (len(waves) + 1),
            out_specs=VMEM,
            input_output_aliases={len(waves) + 1: 0},
            compiler_params=limit(*extra, *([] if whole else waves)),
        )(meta, *on_chip(waves), *on_chip([canvas]))
    message = room((2 * held + 1, size, size), BF16)
    waves = [piece[-1] for piece in late]
    shifted = pltpu.VMEM((2, 3 * size, size), F32)
    outer, canvas = pl.pallas_call(
        functools.partial(
            outer_kernel, areas, columns, held, size, whole, [piece[:3] for piece in late]
        ),
        out_shape=(message, band),
        in_specs=[SMEM] + [VMEM] * (len(waves) + 1),
        out_specs=(VMEM, VMEM),
        scratch_shapes=[shifted],
        input_output_aliases={len(waves) + 1: 1},
        compiler_params=limit(*extra),
        name="band_outer",
    )(meta, *on_chip(waves), *on_chip([canvas]))
    pairs = [(i, i + 1) for i in range(1, areas - 1, 2)]
    outer = lax.ppermute(outer, "area", pairs + [(b, a) for a, b in pairs])
    paired, own = pl.pallas_call(
        functools.partial(paired_kernel, areas, columns, held, size),
        out_shape=(message, room((2 * held + 2, size, size), F32)),
        in_specs=[SMEM, VMEM],
        out_specs=(VMEM, VMEM),
        scratch_shapes=[shifted],
        compiler_params=limit(*extra),
        name="band_paired",
    )(meta, *on_chip([canvas]))
    pairs = [(i, i + 1) for i in range(0, areas - 1, 2)]
    paired = lax.ppermute(paired, "area", pairs + [(b, a) for a, b in pairs])

    rows = pltpu.VMEM((held * size, 2 * size), BF16)
    proj = pltpu.VMEM((held, 2, size, size), F32)
    return pl.pallas_call(
        functools.partial(final_kernel, held, size),
        out_shape=(
            jax.ShapeDtypeStruct((held, 2, size, size), BF16),
            jax.ShapeDtypeStruct((2, size, size), F32),
        ),
        in_specs=[VMEM] * 9,
        out_specs=(VMEM, VMEM),
        scratch_shapes=[rows, rows, proj],
        compiler_params=limit(rows, rows, proj, proj, proj, proj, proj),
        name="relax",
    )(
        *on_chip([own, outer, paired, share, exit_wave, amplitude, probe]),
        *on_chip(twiddles(size)),
    )


def groups_of(pieces):
    at = {(kind, first): piece for piece in pieces for kind, first in [piece[:2]]}
    if len(pieces) == 10:
        half = pieces[-1][1]
        order = [
            [((0, False), 0), ((0, True), 0), ((1, False), 0), ((2, False), 0)],
            [((1, True), 0), ((2, True), 0), ((3, False), 0), ((3, False), half)],
            [((3, True), 0), ((3, True), half)],
        ]
        return [[at[key] for key in group] for group in order]
    return [pieces[first : first + 4] for first in range(0, len(pieces), 4)]


def solution(mesh):
    return jax.shard_map(
        body,
        mesh=mesh,
        in_specs=(
            P(("area", "pos"), None, None, None),
            P(("area", "pos"), None, None),
            P(),
            P(("area", "pos"), None),
            P(("area", "pos"), None),
        ),
        out_specs=(P(("area", "pos"), None, None, None), P(None, "area", "pos")),
        check_vma=False,
    )
```

```python
import functools
import math

import jax
import jax.numpy as jnp
import numpy as np
from jax import lax
from jax.experimental import pallas as pl
from jax.experimental.pallas import tpu as pltpu
from jax.sharding import PartitionSpec as P


F32 = jnp.float32
BF16 = jnp.bfloat16
VMEM = pl.BlockSpec(memory_space=pltpu.VMEM)
SMEM = pl.BlockSpec(memory_space=pltpu.SMEM)


def lanes_of(rows, size):
    return lax.broadcasted_iota(jnp.int32, (rows, size), 1)


def where_is(meta, device, number):
    return tuple(meta[device, 3 * number + part] for part in range(3))


def place(canvas, tile, channel, row, col, data):
    size = data.shape[0]
    turned = pltpu.roll(data, col, 1)
    wraps = lanes_of(size, size) < col
    rows = pl.ds(row, size)
    canvas[tile, channel, rows, :] += jnp.where(wraps, 0.0, turned)
    canvas[tile + 1, channel, rows, :] += jnp.where(wraps, turned, 0.0)


def cut(canvas, tile, channel, row, col, size):
    rows = pl.ds(row, size)
    here = canvas[tile, channel, rows, :]
    after = canvas[tile + 1, channel, rows, :]
    both = jnp.where(lanes_of(size, size) < col, after, here)
    return pltpu.roll(both, lax.rem(size - col, size), 1)


def tile_part(canvas, tile, channel, row, count, size):
    here = canvas[tile, channel, pl.ds(row, count), :]
    after = canvas[tile + 1, channel, pl.ds(row, count), :]
    half = size // 2
    return pltpu.roll(jnp.where(lanes_of(count, size) < half, after, here), half, 1)


def stage_kernel(held, size, offsets, owner, probe, wave, payload):
    for number in range(held):
        for channel, part in enumerate(weighted(probe, wave[number, 0], wave[number, 1])):
            first = (2 * number + channel) * size
            payload[first : first + size, :] = part
    rows = payload.shape[0] - 2 * held * size
    row_at = lax.broadcasted_iota(jnp.int32, (rows, size), 0)
    col_at = lanes_of(rows, size)
    tail = jnp.zeros((rows, size), jnp.int32)
    for number in range(held):
        for part, value in enumerate((offsets[0, number], offsets[1, number], owner[0, number])):
            tail = jnp.where((row_at == number) & (col_at == part), value, tail)
    payload[2 * held * size :, :] = tail.astype(F32).astype(BF16)


def halve_kernel(payload, *halves):
    first = 0
    for half in halves:
        half[...] = payload[first : first + half.shape[0], :]
        first += half.shape[0]


def add_waves(canvas, size, wave, first, count, where, probe=None):
    def add_one(number, carry):
        row, col, tile = where(first + number)
        if probe is None:
            for channel in (0, 1):
                at = pl.multiple_of((2 * number + channel) * size, size)
                place(canvas, tile, channel, row, col, wave[pl.ds(at, size), :].astype(F32))
        else:
            parts = weighted(probe, wave[number, 0], wave[number, 1])
            for channel, part in enumerate(parts):
                place(canvas, tile, channel, row, col, part.astype(F32))
        return carry

    lax.fori_loop(0, count, add_one, 0, unroll=count <= 4)


def weighted(probe, wave_re, wave_im):
    wave_re = wave_re.astype(F32)
    wave_im = wave_im.astype(F32)
    first = probe[0] * wave_re + probe[1] * wave_im
    second = probe[0] * wave_im - probe[1] * wave_re
    return (first.astype(BF16), second.astype(BF16))


def place_by_tail(canvas, held, size, waves, numbers, scalars, sem):
    for at, wave in enumerate(waves):
        numbers[at] = wave[2 * held * size :, :].astype(F32).astype(jnp.int32)
    copy = pltpu.make_async_copy(numbers, scalars, sem)
    copy.start()
    copy.wait()
    for at, wave in enumerate(waves):
        add_waves(
            canvas,
            size,
            wave,
            0,
            held,
            lambda number, at=at: tuple(scalars[at, number, part] for part in range(3)),
        )


def place_by_meta(canvas, columns, size, meta, probe, specs, waves):
    inner = 2 if columns % 2 == 0 else 1
    base = lax.axis_index("area") * columns
    for (kind, first, count), wave in zip(specs, waves):
        source = base + source_of(lax.axis_index("pos"), kind, inner, columns)
        add_waves(
            canvas,
            size,
            wave,
            first,
            count,
            lambda number, source=source: where_is(meta, source, number),
            probe if len(wave.shape) == 4 else None,
        )


def source_of(pos, kind, inner, columns):
    step, swapped = kind
    line = pos // inner
    lines = columns // inner
    if lines & (lines - 1) == 0:
        line = jnp.bitwise_xor(line, step)
    else:
        line = lax.rem(line + lines - step, lines)
    side = lax.rem(pos, inner)
    return line * inner + (inner - 1 - side if swapped else side)


def place_powers(canvas, meta, probe, area, shift, columns, held, size):
    power = probe[0] * probe[0] + probe[1] * probe[1]

    @pl.loop(0, columns)
    def _(source):
        for number in range(held):
            row, col, tile = where_is(meta, area * columns + source, number)
            place(canvas, tile, 0, row + (shift + 1) * size, col, power)


def powers_kernel(columns, held, size, meta, probe, canvas):
    canvas[...] = jnp.zeros_like(canvas)
    place_powers(canvas, meta, probe, lax.axis_index("area"), 0, columns, held, size)


def denominators(areas, columns, held, size, whole, meta, probe, given, share, canvas):
    area = lax.axis_index("area")
    pos = lax.axis_index("pos")
    if not whole:
        canvas[...] = given[...]
    for shift in (-1, 1):
        other = area + shift

        @pl.when((other >= 0) & (other < areas))
        def _(other=other, shift=shift):
            place_powers(canvas, meta, probe, other, shift, columns, held, size)

    half = size // 2
    row_at = lax.broadcasted_iota(jnp.int32, (size, size), 0)
    col_at = lanes_of(size, size)
    for number in range(held):
        row, col, tile = where_is(meta, area * columns + pos, number)
        top = area * size + row - half
        start = tile * size + col - half
        inside = (
            (row_at >= -top)
            & (row_at < areas * size - top)
            & (col_at >= -start)
            & (col_at < columns * size - start)
        )
        sums = cut(canvas, tile, 0, row + size, col, size)
        share[number] = jnp.where(inside, 1.0 / (sums + 0.1), 0.0)
    share[held] = 1.0 / (tile_part(canvas, pos, 0, size + half, size, size) + 0.1)


def first_kernel(held, size, *refs):
    canvas, numbers, scalars, sem = refs[-4:]
    canvas[...] = jnp.zeros_like(canvas)
    place_by_tail(canvas, held, size, refs[:-4], numbers, scalars, sem)


def band_kernel(columns, size, whole, specs, meta, probe, *refs):
    given, canvas = refs[-2:]
    if not whole:
        canvas[...] = given[...]
    place_by_meta(canvas, columns, size, meta, probe, specs, refs[:-2])


def outer_kernel(areas, columns, held, size, whole, specs, meta, *refs):
    given, out, canvas, shifted = refs[-4:]
    if not whole:
        canvas[...] = given[...]
    place_by_meta(canvas, columns, size, meta, None, specs, refs[:-4])
    cut_message(areas, columns, held, size, meta, canvas, out, shifted, True)


def paired_kernel(areas, columns, held, size, meta, canvas, out, own, shifted):
    cut_message(areas, columns, held, size, meta, canvas, out, shifted, False)
    own_sums(columns, held, size, meta, canvas, own)


def neighbour(area, outer):
    step = 1 - 2 * lax.rem(area, 2)
    return -step if outer else step


def cut_message(areas, columns, held, size, meta, canvas, out, shifted, is_outer):
    area = lax.axis_index("area")
    pos = lax.axis_index("pos")
    half = size // 2
    for side in (0, 1):
        shifted[side, :size] = jnp.zeros((size, size), F32)
        shifted[side, 2 * size :] = jnp.zeros((size, size), F32)
    step = neighbour(area, is_outer)
    above = step < 0
    device = jnp.clip(area + step, 0, areas - 1) * columns + pos
    block = pl.multiple_of(jnp.where(above, 0, size), 8)
    for number in range(held):
        row, col, tile = where_is(meta, device, number)
        for channel in (0, 1):
            shifted[channel, size : 2 * size] = cut(canvas, tile, channel, block, col, size)
            first = jnp.where(above, row, row + size)
            out[2 * number + channel] = shifted[channel, pl.ds(first, size), :].astype(BF16)
    first = pl.multiple_of(jnp.where(above, 0, size + half), 8)
    for channel in (0, 1):
        out[2 * held, channel * half : (channel + 1) * half] = tile_part(
            canvas, pos, channel, first, half, size
        ).astype(BF16)


def own_sums(columns, held, size, meta, canvas, own):
    pos = lax.axis_index("pos")
    me = lax.axis_index("area") * columns + pos
    for number in range(held):
        row, col, tile = where_is(meta, me, number)
        for channel in (0, 1):
            own[2 * number + channel] = cut(canvas, tile, channel, row, col, size)
    for channel in (0, 1):
        own[2 * held + channel] = tile_part(canvas, pos, channel, size // 2, size, size)


def split(value):
    high = value.astype(BF16)
    return (high, (value - high.astype(F32)).astype(BF16))


def dot(left, right):
    return jnp.dot(left, right, preferred_element_type=F32)


def from_right(high, low, matrix):
    size = matrix.shape[1]
    if low is None:
        return dot(jnp.concatenate([high, high], 1), matrix[: 2 * size])
    return dot(jnp.concatenate([high, high, low], 1), matrix)


def from_left(matrix, high, low):
    size = matrix.shape[0]
    if low is None:
        return dot(matrix[:, : 2 * size], jnp.concatenate([high, high], 0))
    return dot(matrix, jnp.concatenate([high, high, low], 0))


def there(rows_high, rows_low, right, left, held, size, chunk):
    results = []
    for first in range(0, held, chunk):
        count = min(chunk, held - first)
        at = slice(first * size, (first + count) * size)
        low = None if rows_low is None else rows_low[at, :]
        mid = to_columns(from_right(rows_high[at, :], low, right), count, size)
        high = mid.astype(BF16)
        low = None if rows_low is None else (mid - high.astype(F32)).astype(BF16)
        results.append(from_left(left, high, low))
    return jnp.concatenate(results, 1)


def to_columns(value, held, size):
    return jnp.concatenate(
        [
            jnp.concatenate(
                [
                    value[number * size : (number + 1) * size, part * size : (part + 1) * size]
                    for number in range(held)
                ],
                1,
            )
            for part in (0, 1)
        ],
        0,
    )


def final_kernel(held, size, *refs):
    own, outer, paired, share, wave, amplitude, probe, right, left = refs[:9]
    new_wave, tile_out, rows_high, rows_low, proj = refs[9:]
    half = size // 2
    odd = lax.rem(lax.axis_index("area"), 2) == 1
    scale = share[held]
    for channel in (0, 1):
        rows = slice(channel * half, (channel + 1) * half)
        sums = own[2 * held + channel]
        one = outer[2 * held, rows].astype(F32)
        two = paired[2 * held, rows].astype(F32)
        sums = sums + jnp.concatenate([jnp.where(odd, two, one), jnp.where(odd, one, two)], 0)
        tile_out[channel] = sums * scale
    probe_re = probe[0]
    probe_im = probe[1]
    for number in range(held):
        patch = []
        for channel in (0, 1):
            at = 2 * number + channel
            sums = own[at] + (outer[at].astype(F32) + paired[at].astype(F32))
            patch.append((sums * share[number]).astype(BF16).astype(F32))
        proj_re = probe_re * patch[0] - probe_im * patch[1]
        proj_im = probe_re * patch[1] + probe_im * patch[0]
        proj[number, 0] = proj_re
        proj[number, 1] = proj_im
        at = slice(number * size, (number + 1) * size)
        for channel, part in ((0, proj_re), (1, proj_im)):
            high, low = split(2.0 * part - wave[number, channel].astype(F32))
            rows_high[at, channel * size : (channel + 1) * size] = high
            rows_low[at, channel * size : (channel + 1) * size] = low
    spectrum = there(rows_high, rows_low, right[0], left[0], held, size, CHUNK)
    for number in range(held):
        at = slice(number * size, (number + 1) * size)
        spec_re = spectrum[:size, at]
        spec_im = spectrum[size:, at]
        ratio = amplitude[number].astype(F32) * lax.rsqrt(
            spec_re * spec_re + spec_im * spec_im + 0.01
        )
        for channel, part in ((0, spec_re), (1, spec_im)):
            high, low = split(part * ratio)
            rows_high[at, channel * size : (channel + 1) * size] = high
            rows_low[at, channel * size : (channel + 1) * size] = low
    back = there(rows_high, rows_low, right[1], left[1], held, size, CHUNK)
    for number in range(held):
        at = slice(number * size, (number + 1) * size)
        for channel in (0, 1):
            new_wave[number, channel] = (
                0.75 * wave[number, channel].astype(F32)
                - 0.5 * proj[number, channel]
                + 0.75 * back[channel * size : (channel + 1) * size, at]
            ).astype(BF16)


def twiddles(size):
    at = np.arange(size)
    angle = 2.0 * math.pi * ((at[:, None] * at[None, :]) % size) / size
    real = np.cos(angle) / math.sqrt(size)
    imag = -np.sin(angle) / math.sqrt(size)

    def parts(whole, axis):
        whole = whole.astype(np.float32)
        high = whole.astype(BF16)
        low = (whole - high.astype(np.float32)).astype(BF16)
        return np.concatenate([high, low, high], axis)

    right = [parts(np.block([[real, im], [-im, real]]), 0) for im in (imag, -imag)]
    left = [parts(np.block([[real, -im], [im, real]]), 1) for im in (imag, -imag)]
    return (jnp.asarray(np.stack(right)), jnp.asarray(np.stack(left)))


def steps_of(lines):
    return sorted(range(1, lines), key=lambda step: (step != lines // 2, step))


def gathered(raw, payload, halves, held, columns):
    inner = 2 if columns % 2 == 0 else 1
    lines = columns // inner
    xor = lines & (lines - 1) == 0
    steps = [0] + steps_of(lines)
    pieces = []

    def send(kind, parts, pairs):
        for first, count, value in parts:
            moved = lax.ppermute(value, "pos", pairs)
            pieces.append((kind, first, count, moved))

    for step in steps:
        pairs = [
            (i, (i // inner ^ step if xor else (i // inner + step) % lines) * inner + i % inner)
            for i in range(columns)
        ]
        parts = halves if step == steps[-1] else [(0, held, raw if step == steps[1] else payload)]
        if step == 0:
            pieces.append(((0, False), 0, held, payload))
        else:
            send((step, False), parts, pairs)
    if inner == 2:
        pairs = [(i, i ^ 1) for i in range(columns)]
        for kind, *part in list(pieces):
            if xor and lines > 2 and kind[0] == 1:
                along = [(i, (i // inner ^ 1) * inner + i % inner) for i in range(columns)]
                moved = lax.ppermute(beside, "pos", along)
                pieces.append(((1, True), 0, held, moved))
                continue
            moved = lax.ppermute(part[2], "pos", pairs)
            if kind[0] == 0:
                beside = moved
            pieces.append(((kind[0], True), part[0], part[1], moved))
    return pieces


def on_chip(values):
    if sum(value.size * value.dtype.itemsize for value in values) > 2**23:
        return list(values)
    return [pltpu.with_memory_space_constraint(value, pltpu.VMEM) for value in values]


def limit(*values):
    held = sum(math.prod(value.shape) * np.dtype(value.dtype).itemsize for value in values)
    return pltpu.CompilerParams(vmem_limit_bytes=min(held + 2**23, 60 * 2**20))


SMALL = 6 * 2**20
CHUNK = 2


def room(shape, dtype):
    if math.prod(shape) * np.dtype(dtype).itemsize <= SMALL:
        return pltpu.VMEM(shape, dtype)
    return jax.ShapeDtypeStruct(shape, dtype)


def body(exit_wave, amplitude, probe, offsets, owner):
    areas = lax.axis_size("area")
    columns = lax.axis_size("pos")
    held = exit_wave.shape[0]
    size = exit_wave.shape[-1]
    tail = -(-held // 16) * 16
    cuts = [count for count in (held // 2, held - held // 2) if count]
    payload = pl.pallas_call(
        functools.partial(stage_kernel, held, size),
        out_shape=room((2 * held * size + tail, size), BF16),
        in_specs=[SMEM, SMEM, VMEM, VMEM],
        out_specs=VMEM,
        compiler_params=limit(probe, exit_wave),
        name="stage",
    )(
        *[
            pltpu.with_memory_space_constraint(value, pltpu.HBM)
            for value in (offsets.T, owner.T, probe, exit_wave)
        ]
    )
    halves = pl.pallas_call(
        halve_kernel,
        out_shape=[room((2 * count * size, size), BF16) for count in cuts],
        in_specs=[VMEM],
        out_specs=[VMEM] * len(cuts),
        compiler_params=limit(payload, payload),
        name="halve",
    )(payload)
    firsts = [0, cuts[0]]
    pieces = gathered(exit_wave, payload, list(zip(firsts, cuts, halves)), held, columns)
    mine = jnp.concatenate([offsets, owner], 1).reshape(1, 1, 3 * held)
    meta = lax.all_to_all(
        jnp.broadcast_to(mine, (areas * columns, 1, 3 * held)),
        ("area", "pos"),
        split_axis=0,
        concat_axis=0,
        tiled=True,
    ).reshape(areas * columns, 3 * held)

    powers = room((columns + 1, 1, 4 * size, size), F32)
    whole = not isinstance(powers, jax.ShapeDtypeStruct)
    far_probe = pltpu.with_memory_space_constraint(probe, pltpu.HBM)
    weights = pl.pallas_call(
        functools.partial(powers_kernel, columns, held, size),
        out_shape=powers,
        in_specs=[SMEM, VMEM],
        out_specs=VMEM,
        compiler_params=limit(*([] if whole else [powers])),
        name="powers",
    )(meta, far_probe)
    share, _ = pl.pallas_call(
        functools.partial(denominators, areas, columns, held, size, whole),
        out_shape=(room((held + 1, size, size), F32), powers),
        in_specs=[SMEM, VMEM, VMEM],
        out_specs=(VMEM, VMEM),
        input_output_aliases={2: 1},
        compiler_params=limit(*([] if whole else [powers, powers])),
        name="denominators",
    )(meta, far_probe, *on_chip([weights]))

    band = room((columns + 1, 2, 2 * size, size), F32)
    whole = not isinstance(band, jax.ShapeDtypeStruct)

    extra = [] if whole else [band, band]
    first, *groups, late = groups_of(pieces)
    waves = [piece[-1] for piece in first]
    canvas = pl.pallas_call(
        functools.partial(first_kernel, held, size),
        out_shape=band,
        in_specs=[VMEM] * len(waves),
        out_specs=VMEM,
        scratch_shapes=[
            pltpu.VMEM((len(waves), tail, size), jnp.int32),
            pltpu.SMEM((len(waves), tail, size), jnp.int32),
            pltpu.SemaphoreType.DMA,
        ],
        compiler_params=limit(*extra, *([] if whole else waves)),
        name="band0",
    )(*on_chip(waves))
    for group in groups:
        waves = [piece[-1] for piece in group]
        canvas = pl.pallas_call(
            functools.partial(band_kernel, columns, size, whole, [piece[:3] for piece in group]),
            out_shape=band,
            in_specs=[SMEM] + [VMEM] * (len(waves) + 2),
            out_specs=VMEM,
            input_output_aliases={len(waves) + 2: 0},
            compiler_params=limit(*extra, probe, *([] if whole else waves)),
        )(meta, far_probe, *on_chip(waves), *on_chip([canvas]))
    message = room((2 * held + 1, size, size), BF16)
    waves = [piece[-1] for piece in late]
    shifted = pltpu.VMEM((2, 3 * size, size), F32)
    outer, canvas = pl.pallas_call(
        functools.partial(
            outer_kernel, areas, columns, held, size, whole, [piece[:3] for piece in late]
        ),
        out_shape=(message, band),
        in_specs=[SMEM] + [VMEM] * (len(waves) + 1),
        out_specs=(VMEM, VMEM),
        scratch_shapes=[shifted],
        input_output_aliases={len(waves) + 1: 1},
        compiler_params=limit(*extra),
        name="band_outer",
    )(meta, *on_chip(waves), *on_chip([canvas]))
    pairs = [(i, i + 1) for i in range(1, areas - 1, 2)]
    outer = lax.ppermute(outer, "area", pairs + [(b, a) for a, b in pairs])
    paired, own = pl.pallas_call(
        functools.partial(paired_kernel, areas, columns, held, size),
        out_shape=(message, room((2 * held + 2, size, size), F32)),
        in_specs=[SMEM, VMEM],
        out_specs=(VMEM, VMEM),
        scratch_shapes=[shifted],
        compiler_params=limit(*extra),
        name="band_paired",
    )(meta, *on_chip([canvas]))
    pairs = [(i, i + 1) for i in range(0, areas - 1, 2)]
    paired = lax.ppermute(paired, "area", pairs + [(b, a) for a, b in pairs])

    rows = pltpu.VMEM((held * size, 2 * size), BF16)
    proj = pltpu.VMEM((held, 2, size, size), F32)
    return pl.pallas_call(
        functools.partial(final_kernel, held, size),
        out_shape=(
            jax.ShapeDtypeStruct((held, 2, size, size), BF16),
            jax.ShapeDtypeStruct((2, size, size), F32),
        ),
        in_specs=[VMEM] * 9,
        out_specs=(VMEM, VMEM),
        scratch_shapes=[rows, rows, proj],
        compiler_params=limit(rows, rows, proj, proj, proj, proj, proj),
        name="relax",
    )(
        *on_chip([own, outer, paired, share, exit_wave, amplitude, probe]),
        *on_chip(twiddles(size)),
    )


def groups_of(pieces):
    at = {(kind, first): piece for piece in pieces for kind, first in [piece[:2]]}
    if len(pieces) == 10:
        half = pieces[-1][1]
        order = [
            [((0, False), 0), ((0, True), 0), ((1, False), 0)],
            [((2, False), 0), ((1, True), 0), ((2, True), 0), ((3, False), 0), ((3, False), half)],
            [((3, True), 0), ((3, True), half)],
        ]
        return [[at[key] for key in group] for group in order]
    return [pieces[:1]] + [pieces[first : first + 4] for first in range(1, len(pieces), 4)]


def solution(mesh):
    return jax.shard_map(
        body,
        mesh=mesh,
        in_specs=(
            P(("area", "pos"), None, None, None),
            P(("area", "pos"), None, None),
            P(),
            P(("area", "pos"), None),
            P(("area", "pos"), None),
        ),
        out_specs=(P(("area", "pos"), None, None, None), P(None, "area", "pos")),
        check_vma=False,
    )
```

```python
import functools
import math

import jax
import jax.numpy as jnp
import numpy as np
from jax import lax
from jax.experimental import pallas as pl
from jax.experimental.pallas import tpu as pltpu
from jax.sharding import PartitionSpec as P


F32 = jnp.float32
BF16 = jnp.bfloat16
VMEM = pl.BlockSpec(memory_space=pltpu.VMEM)
SMEM = pl.BlockSpec(memory_space=pltpu.SMEM)


def lanes_of(rows, size):
    return lax.broadcasted_iota(jnp.int32, (rows, size), 1)


def where_is(meta, device, number):
    return tuple(meta[device, 3 * number + part] for part in range(3))


def place(canvas, tile, channel, row, col, data):
    size = data.shape[0]
    turned = pltpu.roll(data, col, 1)
    wraps = lanes_of(size, size) < col
    rows = pl.ds(row, size)
    canvas[tile, channel, rows, :] += jnp.where(wraps, 0.0, turned)
    canvas[tile + 1, channel, rows, :] += jnp.where(wraps, turned, 0.0)


def cut(canvas, tile, channel, row, col, size):
    rows = pl.ds(row, size)
    here = canvas[tile, channel, rows, :]
    after = canvas[tile + 1, channel, rows, :]
    both = jnp.where(lanes_of(size, size) < col, after, here)
    return pltpu.roll(both, lax.rem(size - col, size), 1)


def tile_part(canvas, tile, channel, row, count, size):
    here = canvas[tile, channel, pl.ds(row, count), :]
    after = canvas[tile + 1, channel, pl.ds(row, count), :]
    half = size // 2
    return pltpu.roll(jnp.where(lanes_of(count, size) < half, after, here), half, 1)


def stage_kernel(held, size, offsets, owner, probe, wave, payload):
    for number in range(held):
        for channel, part in enumerate(weighted(probe, wave[number, 0], wave[number, 1])):
            first = (2 * number + channel) * size
            payload[first : first + size, :] = part
    rows = payload.shape[0] - 2 * held * size
    row_at = lax.broadcasted_iota(jnp.int32, (rows, size), 0)
    col_at = lanes_of(rows, size)
    tail = jnp.zeros((rows, size), jnp.int32)
    for number in range(held):
        for part, value in enumerate((offsets[0, number], offsets[1, number], owner[0, number])):
            tail = jnp.where((row_at == number) & (col_at == part), value, tail)
    payload[2 * held * size :, :] = tail.astype(F32).astype(BF16)


def halve_kernel(payload, *halves):
    first = 0
    for half in halves:
        half[...] = payload[first : first + half.shape[0], :]
        first += half.shape[0]


def add_waves(canvas, size, wave, first, count, where, probe=None):
    def add_one(number, carry):
        row, col, tile = where(first + number)
        if probe is None:
            for channel in (0, 1):
                at = pl.multiple_of((2 * number + channel) * size, size)
                place(canvas, tile, channel, row, col, wave[pl.ds(at, size), :].astype(F32))
        else:
            parts = weighted(probe, wave[number, 0], wave[number, 1])
            for channel, part in enumerate(parts):
                place(canvas, tile, channel, row, col, part.astype(F32))
        return carry

    lax.fori_loop(0, count, add_one, 0, unroll=count <= 4)


def weighted(probe, wave_re, wave_im):
    wave_re = wave_re.astype(F32)
    wave_im = wave_im.astype(F32)
    first = probe[0] * wave_re + probe[1] * wave_im
    second = probe[0] * wave_im - probe[1] * wave_re
    return (first.astype(BF16), second.astype(BF16))


def place_by_tail(canvas, held, size, waves, numbers, scalars, sem):
    for at, wave in enumerate(waves):
        numbers[at] = wave[2 * held * size :, :].astype(F32).astype(jnp.int32)
    copy = pltpu.make_async_copy(numbers, scalars, sem)
    copy.start()
    copy.wait()
    for at, wave in enumerate(waves):
        add_waves(
            canvas,
            size,
            wave,
            0,
            held,
            lambda number, at=at: tuple(scalars[at, number, part] for part in range(3)),
        )


def place_by_meta(canvas, columns, size, meta, probe, specs, waves):
    inner = 2 if columns % 2 == 0 else 1
    base = lax.axis_index("area") * columns
    for (kind, first, count), wave in zip(specs, waves):
        source = base + source_of(lax.axis_index("pos"), kind, inner, columns)
        add_waves(
            canvas,
            size,
            wave,
            first,
            count,
            lambda number, source=source: where_is(meta, source, number),
            probe if len(wave.shape) == 4 else None,
        )


def source_of(pos, kind, inner, columns):
    step, swapped = kind
    line = pos // inner
    lines = columns // inner
    if lines & (lines - 1) == 0:
        line = jnp.bitwise_xor(line, step)
    else:
        line = lax.rem(line + lines - step, lines)
    side = lax.rem(pos, inner)
    return line * inner + (inner - 1 - side if swapped else side)


def place_powers(canvas, meta, probe, area, shift, columns, held, size):
    power = probe[0] * probe[0] + probe[1] * probe[1]

    @pl.loop(0, columns, unroll=4)
    def _(source):
        for number in range(held):
            row, col, tile = where_is(meta, area * columns + source, number)
            place(canvas, tile, 0, row + (shift + 1) * size, col, power)


def powers_kernel(columns, held, size, meta, probe, canvas):
    canvas[...] = jnp.zeros_like(canvas)
    place_powers(canvas, meta, probe, lax.axis_index("area"), 0, columns, held, size)


def denominators(areas, columns, held, size, whole, meta, probe, given, share, canvas):
    area = lax.axis_index("area")
    pos = lax.axis_index("pos")
    if not whole:
        canvas[...] = given[...]
    for shift in (-1, 1):
        other = area + shift

        @pl.when((other >= 0) & (other < areas))
        def _(other=other, shift=shift):
            place_powers(canvas, meta, probe, other, shift, columns, held, size)

    half = size // 2
    row_at = lax.broadcasted_iota(jnp.int32, (size, size), 0)
    col_at = lanes_of(size, size)
    for number in range(held):
        row, col, tile = where_is(meta, area * columns + pos, number)
        top = area * size + row - half
        start = tile * size + col - half
        inside = (
            (row_at >= -top)
            & (row_at < areas * size - top)
            & (col_at >= -start)
            & (col_at < columns * size - start)
        )
        sums = cut(canvas, tile, 0, row + size, col, size)
        share[number] = jnp.where(inside, 1.0 / (sums + 0.1), 0.0)
    share[held] = 1.0 / (tile_part(canvas, pos, 0, size + half, size, size) + 0.1)


def first_kernel(held, size, *refs):
    canvas, numbers, scalars, sem = refs[-4:]
    canvas[...] = jnp.zeros_like(canvas)
    place_by_tail(canvas, held, size, refs[:-4], numbers, scalars, sem)


def band_kernel(columns, size, whole, specs, meta, probe, *refs):
    given, canvas = refs[-2:]
    if not whole:
        canvas[...] = given[...]
    place_by_meta(canvas, columns, size, meta, probe, specs, refs[:-2])


def band_and_powers_kernel(columns, held, size, specs, meta, probe, *refs):
    weights = refs[-1]
    band_kernel(columns, size, True, specs, meta, probe, *refs[:-1])
    powers_kernel(columns, held, size, meta, probe, weights)


def outer_kernel(areas, columns, held, size, whole, specs, meta, *refs):
    given, out, canvas, shifted = refs[-4:]
    if not whole:
        canvas[...] = given[...]
    place_by_meta(canvas, columns, size, meta, None, specs, refs[:-4])
    cut_message(areas, columns, held, size, meta, canvas, out, shifted, True)


def paired_kernel(areas, columns, held, size, meta, canvas, out, own, shifted):
    cut_message(areas, columns, held, size, meta, canvas, out, shifted, False)
    own_sums(columns, held, size, meta, canvas, own)


def neighbour(area, outer):
    step = 1 - 2 * lax.rem(area, 2)
    return -step if outer else step


def cut_message(areas, columns, held, size, meta, canvas, out, shifted, is_outer):
    area = lax.axis_index("area")
    pos = lax.axis_index("pos")
    half = size // 2
    for side in (0, 1):
        shifted[side, :size] = jnp.zeros((size, size), F32)
        shifted[side, 2 * size :] = jnp.zeros((size, size), F32)
    step = neighbour(area, is_outer)
    above = step < 0
    device = jnp.clip(area + step, 0, areas - 1) * columns + pos
    block = pl.multiple_of(jnp.where(above, 0, size), 8)
    for number in range(held):
        row, col, tile = where_is(meta, device, number)
        for channel in (0, 1):
            shifted[channel, size : 2 * size] = cut(canvas, tile, channel, block, col, size)
            first = jnp.where(above, row, row + size)
            out[2 * number + channel] = shifted[channel, pl.ds(first, size), :].astype(BF16)
    first = pl.multiple_of(jnp.where(above, 0, size + half), 8)
    for channel in (0, 1):
        out[2 * held, channel * half : (channel + 1) * half] = tile_part(
            canvas, pos, channel, first, half, size
        ).astype(BF16)


def own_sums(columns, held, size, meta, canvas, own):
    pos = lax.axis_index("pos")
    me = lax.axis_index("area") * columns + pos
    for number in range(held):
        row, col, tile = where_is(meta, me, number)
        for channel in (0, 1):
            own[2 * number + channel] = cut(canvas, tile, channel, row, col, size)
    for channel in (0, 1):
        own[2 * held + channel] = tile_part(canvas, pos, channel, size // 2, size, size)


def split(value):
    high = value.astype(BF16)
    return (high, (value - high.astype(F32)).astype(BF16))


def dot(left, right):
    return jnp.dot(left, right, preferred_element_type=F32)


def from_right(high, low, matrix):
    size = matrix.shape[1]
    if low is None:
        return dot(jnp.concatenate([high, high], 1), matrix[: 2 * size])
    return dot(jnp.concatenate([high, high, low], 1), matrix)


def from_left(matrix, high, low):
    size = matrix.shape[0]
    if low is None:
        return dot(matrix[:, : 2 * size], jnp.concatenate([high, high], 0))
    return dot(matrix, jnp.concatenate([high, high, low], 0))


def there(rows_high, rows_low, right, left, held, size, chunk):
    results = []
    for first in range(0, held, chunk):
        count = min(chunk, held - first)
        at = slice(first * size, (first + count) * size)
        low = None if rows_low is None else rows_low[at, :]
        mid = to_columns(from_right(rows_high[at, :], low, right), count, size)
        high = mid.astype(BF16)
        low = None if rows_low is None else (mid - high.astype(F32)).astype(BF16)
        results.append(from_left(left, high, low))
    return jnp.concatenate(results, 1)


def to_columns(value, held, size):
    return jnp.concatenate(
        [
            jnp.concatenate(
                [
                    value[number * size : (number + 1) * size, part * size : (part + 1) * size]
                    for number in range(held)
                ],
                1,
            )
            for part in (0, 1)
        ],
        0,
    )


def final_kernel(held, size, *refs):
    own, outer, paired, share, wave, amplitude, probe, right, left = refs[:9]
    new_wave, tile_out, rows_high, rows_low, proj = refs[9:]
    half = size // 2
    odd = lax.rem(lax.axis_index("area"), 2) == 1
    scale = share[held]
    for channel in (0, 1):
        rows = slice(channel * half, (channel + 1) * half)
        sums = own[2 * held + channel]
        one = outer[2 * held, rows].astype(F32)
        two = paired[2 * held, rows].astype(F32)
        sums = sums + jnp.concatenate([jnp.where(odd, two, one), jnp.where(odd, one, two)], 0)
        tile_out[channel] = sums * scale
    probe_re = probe[0]
    probe_im = probe[1]
    for number in range(held):
        patch = []
        for channel in (0, 1):
            at = 2 * number + channel
            sums = own[at] + (outer[at].astype(F32) + paired[at].astype(F32))
            patch.append((sums * share[number]).astype(BF16).astype(F32))
        proj_re = probe_re * patch[0] - probe_im * patch[1]
        proj_im = probe_re * patch[1] + probe_im * patch[0]
        proj[number, 0] = proj_re
        proj[number, 1] = proj_im
        at = slice(number * size, (number + 1) * size)
        for channel, part in ((0, proj_re), (1, proj_im)):
            high, low = split(2.0 * part - wave[number, channel].astype(F32))
            rows_high[at, channel * size : (channel + 1) * size] = high
            rows_low[at, channel * size : (channel + 1) * size] = low
    spectrum = there(rows_high, rows_low, right[0], left[0], held, size, CHUNK)
    for number in range(held):
        at = slice(number * size, (number + 1) * size)
        spec_re = spectrum[:size, at]
        spec_im = spectrum[size:, at]
        ratio = amplitude[number].astype(F32) * lax.rsqrt(
            spec_re * spec_re + spec_im * spec_im + 0.01
        )
        for channel, part in ((0, spec_re), (1, spec_im)):
            high, low = split(part * ratio)
            rows_high[at, channel * size : (channel + 1) * size] = high
            rows_low[at, channel * size : (channel + 1) * size] = low
    back = there(rows_high, rows_low, right[1], left[1], held, size, CHUNK)
    for number in range(held):
        at = slice(number * size, (number + 1) * size)
        for channel in (0, 1):
            new_wave[number, channel] = (
                0.75 * wave[number, channel].astype(F32)
                - 0.5 * proj[number, channel]
                + 0.75 * back[channel * size : (channel + 1) * size, at]
            ).astype(BF16)


def twiddles(size):
    at = np.arange(size)
    angle = 2.0 * math.pi * ((at[:, None] * at[None, :]) % size) / size
    real = np.cos(angle) / math.sqrt(size)
    imag = -np.sin(angle) / math.sqrt(size)

    def parts(whole, axis):
        whole = whole.astype(np.float32)
        high = whole.astype(BF16)
        low = (whole - high.astype(np.float32)).astype(BF16)
        return np.concatenate([high, low, high], axis)

    right = [parts(np.block([[real, im], [-im, real]]), 0) for im in (imag, -imag)]
    left = [parts(np.block([[real, -im], [im, real]]), 1) for im in (imag, -imag)]
    return (jnp.asarray(np.stack(right)), jnp.asarray(np.stack(left)))


def steps_of(lines):
    return sorted(range(1, lines), key=lambda step: (step != lines // 2, step))


def gathered(raw, payload, halves, held, columns):
    inner = 2 if columns % 2 == 0 else 1
    lines = columns // inner
    xor = lines & (lines - 1) == 0
    steps = [0] + steps_of(lines)
    pieces = []

    def send(kind, parts, pairs):
        for first, count, value in parts:
            moved = lax.ppermute(value, "pos", pairs)
            pieces.append((kind, first, count, moved))

    for step in steps:
        pairs = [
            (i, (i // inner ^ step if xor else (i // inner + step) % lines) * inner + i % inner)
            for i in range(columns)
        ]
        parts = halves if step == steps[-1] else [(0, held, raw if step == steps[1] else payload)]
        if step == 0:
            pieces.append(((0, False), 0, held, payload))
        else:
            send((step, False), parts, pairs)
    if inner == 2:
        pairs = [(i, i ^ 1) for i in range(columns)]
        for kind, *part in list(pieces):
            if xor and lines > 2 and kind[0] == 1:
                along = [(i, (i // inner ^ 1) * inner + i % inner) for i in range(columns)]
                moved = lax.ppermute(beside, "pos", along)
                pieces.append(((1, True), 0, held, moved))
                continue
            moved = lax.ppermute(part[2], "pos", pairs)
            if kind[0] == 0:
                beside = moved
            pieces.append(((kind[0], True), part[0], part[1], moved))
    return pieces


def on_chip(values):
    if sum(value.size * value.dtype.itemsize for value in values) > 2**23:
        return list(values)
    return [pltpu.with_memory_space_constraint(value, pltpu.VMEM) for value in values]


def limit(*values):
    held = sum(math.prod(value.shape) * np.dtype(value.dtype).itemsize for value in values)
    return pltpu.CompilerParams(vmem_limit_bytes=min(held + 2**23, 60 * 2**20))


SMALL = 6 * 2**20
CHUNK = 2


def room(shape, dtype):
    if math.prod(shape) * np.dtype(dtype).itemsize <= SMALL:
        return pltpu.VMEM(shape, dtype)
    return jax.ShapeDtypeStruct(shape, dtype)


def body(exit_wave, amplitude, probe, offsets, owner):
    areas = lax.axis_size("area")
    columns = lax.axis_size("pos")
    held = exit_wave.shape[0]
    size = exit_wave.shape[-1]
    tail = -(-held // 16) * 16
    cuts = [count for count in (held // 2, held - held // 2) if count]
    payload = pl.pallas_call(
        functools.partial(stage_kernel, held, size),
        out_shape=room((2 * held * size + tail, size), BF16),
        in_specs=[SMEM, SMEM, VMEM, VMEM],
        out_specs=VMEM,
        compiler_params=limit(probe, exit_wave),
        name="stage",
    )(
        *[
            pltpu.with_memory_space_constraint(value, pltpu.HBM)
            for value in (offsets.T, owner.T, probe, exit_wave)
        ]
    )
    halves = pl.pallas_call(
        halve_kernel,
        out_shape=[room((2 * count * size, size), BF16) for count in cuts],
        in_specs=[VMEM],
        out_specs=[VMEM] * len(cuts),
        compiler_params=limit(payload, payload),
        name="halve",
    )(payload)
    firsts = [0, cuts[0]]
    pieces = gathered(exit_wave, payload, list(zip(firsts, cuts, halves)), held, columns)
    mine = jnp.concatenate([offsets, owner], 1).reshape(1, 1, 3 * held)
    meta = lax.all_to_all(
        jnp.broadcast_to(mine, (areas * columns, 1, 3 * held)),
        ("area", "pos"),
        split_axis=0,
        concat_axis=0,
        tiled=True,
    ).reshape(areas * columns, 3 * held)

    powers = room((columns + 1, 1, 4 * size, size), F32)
    whole = not isinstance(powers, jax.ShapeDtypeStruct)
    far_probe = pltpu.with_memory_space_constraint(probe, pltpu.HBM)
    band = room((columns + 1, 2, 2 * size, size), F32)
    whole = not isinstance(band, jax.ShapeDtypeStruct)

    extra = [] if whole else [band, band]
    first, *groups, late = groups_of(pieces)
    waves = [piece[-1] for piece in first]
    canvas = pl.pallas_call(
        functools.partial(first_kernel, held, size),
        out_shape=band,
        in_specs=[VMEM] * len(waves),
        out_specs=VMEM,
        scratch_shapes=[
            pltpu.VMEM((len(waves), tail, size), jnp.int32),
            pltpu.SMEM((len(waves), tail, size), jnp.int32),
            pltpu.SemaphoreType.DMA,
        ],
        compiler_params=limit(*extra, *([] if whole else waves)),
        name="band0",
    )(*on_chip(waves))
    if whole:
        *groups, final = groups
        for group in groups:
            waves = [piece[-1] for piece in group]
            canvas = pl.pallas_call(
                functools.partial(band_kernel, columns, size, whole, [piece[:3] for piece in group]),
                out_shape=band,
                in_specs=[SMEM] + [VMEM] * (len(waves) + 2),
                out_specs=VMEM,
                input_output_aliases={len(waves) + 2: 0},
                compiler_params=limit(*extra, probe, *([] if whole else waves)),
            )(meta, far_probe, *on_chip(waves), *on_chip([canvas]))
        waves = [piece[-1] for piece in final]
        specs = [piece[:3] for piece in final]
        count = len(waves) + 2
        canvas, weights = pl.pallas_call(
            functools.partial(band_and_powers_kernel, columns, held, size, specs),
            out_shape=(band, powers),
            in_specs=[SMEM] + [VMEM] * count,
            out_specs=(VMEM, VMEM),
            input_output_aliases={count: 0},
            compiler_params=limit(probe),
            name="band_powers",
        )(meta, far_probe, *on_chip(waves), *on_chip([canvas]))
    else:
        for group in groups:
            waves = [piece[-1] for piece in group]
            canvas = pl.pallas_call(
                functools.partial(band_kernel, columns, size, whole, [piece[:3] for piece in group]),
                out_shape=band,
                in_specs=[SMEM] + [VMEM] * (len(waves) + 2),
                out_specs=VMEM,
                input_output_aliases={len(waves) + 2: 0},
                compiler_params=limit(*extra, probe, *([] if whole else waves)),
            )(meta, far_probe, *on_chip(waves), *on_chip([canvas]))
        weights = pl.pallas_call(
            functools.partial(powers_kernel, columns, held, size),
            out_shape=powers,
            in_specs=[SMEM, VMEM],
            out_specs=VMEM,
            compiler_params=limit(*([] if whole else [powers])),
            name="powers",
        )(meta, far_probe)
    share, _ = pl.pallas_call(
        functools.partial(denominators, areas, columns, held, size, whole),
        out_shape=(room((held + 1, size, size), F32), powers),
        in_specs=[SMEM, VMEM, VMEM],
        out_specs=(VMEM, VMEM),
        input_output_aliases={2: 1},
        compiler_params=limit(*([] if whole else [powers, powers])),
        name="denominators",
    )(meta, far_probe, *on_chip([weights]))

    message = room((2 * held + 1, size, size), BF16)
    waves = [piece[-1] for piece in late]
    shifted = pltpu.VMEM((2, 3 * size, size), F32)
    outer, canvas = pl.pallas_call(
        functools.partial(
            outer_kernel, areas, columns, held, size, whole, [piece[:3] for piece in late]
        ),
        out_shape=(message, band),
        in_specs=[SMEM] + [VMEM] * (len(waves) + 1),
        out_specs=(VMEM, VMEM),
        scratch_shapes=[shifted],
        input_output_aliases={len(waves) + 1: 1},
        compiler_params=limit(*extra),
        name="band_outer",
    )(meta, *on_chip(waves), *on_chip([canvas]))
    pairs = [(i, i + 1) for i in range(1, areas - 1, 2)]
    outer = lax.ppermute(outer, "area", pairs + [(b, a) for a, b in pairs])
    paired, own = pl.pallas_call(
        functools.partial(paired_kernel, areas, columns, held, size),
        out_shape=(message, room((2 * held + 2, size, size), F32)),
        in_specs=[SMEM, VMEM],
        out_specs=(VMEM, VMEM),
        scratch_shapes=[shifted],
        compiler_params=limit(*extra),
        name="band_paired",
    )(meta, *on_chip([canvas]))
    pairs = [(i, i + 1) for i in range(0, areas - 1, 2)]
    paired = lax.ppermute(paired, "area", pairs + [(b, a) for a, b in pairs])

    rows = pltpu.VMEM((held * size, 2 * size), BF16)
    proj = pltpu.VMEM((held, 2, size, size), F32)
    return pl.pallas_call(
        functools.partial(final_kernel, held, size),
        out_shape=(
            jax.ShapeDtypeStruct((held, 2, size, size), BF16),
            jax.ShapeDtypeStruct((2, size, size), F32),
        ),
        in_specs=[VMEM] * 9,
        out_specs=(VMEM, VMEM),
        scratch_shapes=[rows, rows, proj],
        compiler_params=limit(rows, rows, proj, proj, proj, proj, proj),
        name="relax",
    )(
        *on_chip([own, outer, paired, share, exit_wave, amplitude, probe]),
        *on_chip(twiddles(size)),
    )


def groups_of(pieces):
    at = {(kind, first): piece for piece in pieces for kind, first in [piece[:2]]}
    if len(pieces) == 10:
        half = pieces[-1][1]
        order = [
            [((0, False), 0), ((0, True), 0), ((1, False), 0)],
            [((2, False), 0), ((1, True), 0), ((2, True), 0), ((3, False), 0), ((3, False), half)],
            [((3, True), 0), ((3, True), half)],
        ]
        return [[at[key] for key in group] for group in order]
    return [pieces[:1]] + [pieces[first : first + 4] for first in range(1, len(pieces), 4)]


def solution(mesh):
    return jax.shard_map(
        body,
        mesh=mesh,
        in_specs=(
            P(("area", "pos"), None, None, None),
            P(("area", "pos"), None, None),
            P(),
            P(("area", "pos"), None),
            P(("area", "pos"), None),
        ),
        out_specs=(P(("area", "pos"), None, None, None), P(None, "area", "pos")),
        check_vma=False,
    )
```
